128 devices in a mesh: state: 4 (over z_hi, core), row: 32 (over z_lo, x, y).
Axes of the slice: x: 4, y: 4, z: 4 (z_hi: 2, z_lo: 2; z = z_hi * 2 + z_lo), core: 2. Of those that a mesh axis runs over, the one named last changes fastest.
Arguments:
- vectors: bfloat16 [131072, 512], P('row', 'state'), as said below
- active: int32 [8], replicated, may hold values 0 or 1
Outputs:
- orthonormal: bfloat16 [131072, 512], P('row', 'state')
The draws below stay inside these ranges and needn't reach their ends.
Inputs may be any that keep to these rules, and one draw needn't show every extreme that they name: Each row and each column of vectors has its own scale.
All inputs are finite; a program needn't handle non-finite values.
Results may differ from the reference program's by a relative error of at most 0.00096.
Values may be sent and summed in bfloat16 or wider, within the bound.
A program may use at most 64 MiB of HBM per device.

```python
import jax
import jax.numpy as jnp
from jax import lax

STATES = 8
VECS = 64
ITERS = 5
COLS = 512
ROWS = 131072


def draw_vectors(key, part):
    keys = jax.random.split(jax.random.fold_in(key, 11), 4)
    base = jax.random.normal(keys[0], (ROWS, COLS), jnp.float32)
    shuffle = jax.random.permutation(keys[1], COLS)
    mixed = base + 0.5 * base[:, shuffle]
    position = jnp.arange(ROWS).astype(jnp.float32) / ROWS
    ramp = jnp.exp(jnp.log(32.0) * (position - 0.5))
    col_scale = jnp.exp(jax.random.uniform(keys[2], (COLS,), jnp.float32, jnp.log(0.5), jnp.log(2.0)))
    row_scale = jnp.exp(jax.random.uniform(keys[3], (ROWS,), jnp.float32, 0.0, jnp.log(4.0)))
    return (mixed * col_scale[None, :] * (row_scale * ramp)[:, None]).astype(jnp.bfloat16)


def with_ends(values, stream_key, smallest, high):
    place = [jax.random.randint(jax.random.fold_in(stream_key, axis), (), 0, length) for axis, length in enumerate(values.shape)]
    main_axis = values.shape.index(max(values.shape))
    next_to = place[:main_axis] + [(place[main_axis] + 1) % values.shape[main_axis]] + place[main_axis + 1:]
    return values.at[tuple(place)].set(smallest).at[tuple(next_to)].set(high)


def setup_inputs(seed: int = 0) -> dict:
    key_of = jax.random.split(jax.random.key(seed), 3)
    return {
        "vectors": draw_vectors(jax.random.fold_in(key_of[2], 71), 0),
        "active": with_ends((jax.random.randint(key_of[1], (STATES,), 0, 4) < 3).astype(jnp.int32), jax.random.fold_in(key_of[1], 1), 0, 1),
    }


def newton_schulz(gram_matrix):
    identity = jnp.eye(gram_matrix.shape[0], dtype=jnp.float32)
    frob_norm = jnp.sqrt(jnp.sum(gram_matrix * gram_matrix))
    current = gram_matrix / frob_norm
    inverse = identity
    for repeat in range(ITERS):
        newton_step = 0.5 * (3.0 * identity - jnp.dot(inverse, current, precision=lax.Precision.HIGHEST))
        current = jnp.dot(current, newton_step, precision=lax.Precision.HIGHEST)
        inverse = jnp.dot(newton_step, inverse, precision=lax.Precision.HIGHEST)
    return (inverse * jnp.sqrt(ROWS / frob_norm)).astype(jnp.bfloat16)

def reference(vectors, active):
    flag_cols = jnp.repeat(active.astype(jnp.float32), VECS)
    masked = vectors * flag_cols.astype(jnp.bfloat16)
    gram_matrix = lax.dot_general(masked, masked, (((0,), (0,)), ((), ())), preferred_element_type=jnp.float32)
    gram_matrix = gram_matrix + jnp.diag((1.0 - flag_cols) * ROWS)
    factor = newton_schulz(gram_matrix)
    result = jnp.dot(masked, factor, preferred_element_type=jnp.float32)
    result = result + (1.0 - flag_cols) * vectors.astype(jnp.float32)
    return result.astype(jnp.bfloat16)
```

```python
import functools

import jax
import jax.numpy as jnp
from jax import lax
from jax.experimental import pallas as pl
from jax.experimental.pallas import tpu as pltpu
from jax.sharding import PartitionSpec as P

VECS = 64
MESH = pl.DeviceIdType.MESH
F32 = jnp.float32
BF16 = jnp.bfloat16
ANY = pl.BlockSpec(memory_space=pl.ANY)
VMEM = pl.BlockSpec(memory_space=pltpu.VMEM)

HALF, QUARTER, OWN, LINK, RELAY = 0, 1, 5, 6, 10
CORE, XDIM, YDIM, ZDIM, YBACK, XBACK, CBACK = 0, 1, 4, 7, 10, 13, 16
EARLY, LATE, SEMS = 14, 31, 48


def gram(left, right):
    return lax.dot_general(left, right, (((0,), (0,)), ((), ())), preferred_element_type=F32)


def exchange_kernel(
    vec_ref, early_ref, late_ref, rest_ref,
    half, quart, early_part, early_core, early_x, early_y, early_z, early_sum1, early_sum2, early_sum3,
    late_part, late_core, late_x, late_y, late_z, late_sum1, late_sum2, late_sum3,
    local_sem, send_sem, recv_sem,
):
    s, r = lax.axis_index("state"), lax.axis_index("row")
    zh, c = s // 2, s % 2
    zl, x, y = r // 16, (r // 4) % 4, r % 4
    z = zh * 2 + zl
    other_r = r + 16 * (1 - 2 * zl)
    partner = (s + 1 - 2 * c, r)
    rows = vec_ref.shape[0]
    half_rows, quart_rows = rows // 2, rows // 4

    def x_peer(d):
        return (s, zl * 16 + ((x + d) % 4) * 4 + y)

    def y_peer(d):
        return (s, zl * 16 + x * 4 + (y + d) % 4)

    def z_peer(d):
        to = (z + d) % 4
        return ((to // 2) * 2 + c, (to % 2) * 16 + x * 4 + y)

    def send(src, dst, sem, device, recv=None):
        return pltpu.make_async_remote_copy(
            src_ref=src, dst_ref=dst, send_sem=send_sem.at[sem],
            recv_sem=recv_sem.at[sem if recv is None else recv],
            device_id=device, device_id_type=MESH,
        )

    started = []

    def start(copies):
        for copy in copies:
            copy.start()
        started.extend(copies)
        return copies

    def arrive(copies):
        for copy in copies:
            copy.wait_recv()

    mine = pltpu.make_async_copy(vec_ref.at[pl.ds(c * half_rows, half_rows)], half.at[c], local_sem)
    mine.start()

    barrier = pltpu.get_barrier_semaphore()
    peers = [partner] + [(t, other_r) for t in range(4)] + [z_peer(2)]
    peers += [x_peer(d) for d in (1, 2, 3)] + [y_peer(d) for d in (1, 2, 3)]
    for peer in peers:
        pl.semaphore_signal(barrier, inc=1, device_id=peer, device_id_type=MESH)
    pl.semaphore_wait(barrier, len(peers))

    halves = start([send(vec_ref.at[pl.ds((1 - c) * half_rows, half_rows)], half.at[c], HALF, partner)])
    quarters = [
        send(vec_ref.at[pl.ds(t * quart_rows, quart_rows)], quart.at[s], QUARTER + t, (t, other_r), recv=QUARTER + s)
        for t in range(4)
    ]
    start(quarters)

    def quarters_arrive():
        for t in range(4):
            send(vec_ref.at[pl.ds(0, quart_rows)], quart.at[t], QUARTER + t, (t, other_r)).wait_recv()

    def core_step(part, got, base):
        return [send(part.at[pl.ds((1 - c) * 128, 128)], got, base + CORE, partner)]

    def x_step(sum1, got, base):
        return [
            send(sum1.at[pl.ds(((x + d) % 4) * 32, 32)], got.at[d - 1], base + XDIM + d - 1, x_peer(d)) for d in (1, 2, 3)
        ]

    def y_step(sum2, got, base):
        return [
            send(sum2.at[pl.ds(((y + d) % 4) * 8, 8)], got.at[d - 1], base + YDIM + d - 1, y_peer(d)) for d in (1, 2, 3)
        ]

    def z_step(sum3, got, base):
        return [send(sum3, got.at[z], base + ZDIM + d - 1, z_peer(d)) for d in (1, 2, 3)]

    def y_back(out, base):
        return [send(out.at[c, x, y], out.at[c, x, y], base + YBACK + d - 1, y_peer(d)) for d in (1, 2, 3)]

    def x_back(out, base):
        return [send(out.at[c, x], out.at[c, x], base + XBACK + d - 1, x_peer(d)) for d in (1, 2, 3)]

    def core_back(out, base):
        return [send(out.at[c], out.at[c], base + CBACK, partner)]

    mine.wait()
    arrive(halves)
    both = jnp.concatenate([half[0], half[1]], axis=1)
    early_part[...] = gram(both, both)
    step = start(core_step(early_part, early_core, EARLY))
    arrive(step)
    early_sum1[...] = early_part[pl.ds(pl.multiple_of(c * 128, 128), 128), :] + early_core[...]
    step = start(x_step(early_sum1, early_x, EARLY))
    start([send(vec_ref, rest_ref.at[0], OWN, partner)])
    arrive(step)
    early_sum2[...] = early_sum1[pl.ds(pl.multiple_of(x * 32, 32), 32), :] + early_x[0] + early_x[1] + early_x[2]
    step = start(y_step(early_sum2, early_y, EARLY))
    arrive(step)
    early_sum3[...] = early_sum2[pl.ds(pl.multiple_of(y * 8, 8), 8), :] + early_y[0] + early_y[1] + early_y[2]
    early_z[z] = early_sum3[...]

    quarters_arrive()
    early_step = start(z_step(early_sum3, early_z, EARLY))
    left = jnp.concatenate([quart[0], quart[1]], axis=1)
    right = jnp.concatenate([quart[2], quart[3]], axis=1)
    late_part[...] = gram(left, right)
    step = start(core_step(late_part, late_core, LATE))

    def link(part):
        return [
            send(
                quart.at[2 - 2 * to + part],
                rest_ref.at[1 + part, pl.ds(s * quart_rows, quart_rows)],
                LINK + part * 2 + to,
                (to * 2 + c, other_r),
                recv=LINK + part * 2 + zh,
            )
            for to in (0, 1)
        ]

    def link_arrive(part):
        for frm in (0, 1):
            send(
                quart.at[0], rest_ref.at[1 + part, pl.ds((frm * 2 + c) * quart_rows, quart_rows)],
                LINK + part * 2 + frm, partner,
            ).wait_recv()

    def relay(part):
        blocks = [rest_ref.at[1 + part, pl.ds((frm * 2 + c) * quart_rows, quart_rows)] for frm in (0, 1)]
        return [send(block, block, RELAY + part * 2 + frm, partner) for frm, block in enumerate(blocks)]

    def relay_arrive(part):
        blocks = [rest_ref.at[1 + part, pl.ds((frm * 2 + 1 - c) * quart_rows, quart_rows)] for frm in (0, 1)]
        for frm, block in enumerate(blocks):
            send(block, block, RELAY + part * 2 + frm, partner).wait_recv()

    start(link(0))
    arrive(step)
    late_sum1[...] = late_part[pl.ds(pl.multiple_of(c * 128, 128), 128), :] + late_core[...]
    step = start(x_step(late_sum1, late_x, LATE))
    arrive(early_step)
    early_ref[c, x, y, 0] = early_z[0] + early_z[1]
    early_ref[c, x, y, 1] = early_z[2] + early_z[3]
    early_step = start(y_back(early_ref, EARLY))
    arrive(step)
    late_sum2[...] = late_sum1[pl.ds(pl.multiple_of(x * 32, 32), 32), :] + late_x[0] + late_x[1] + late_x[2]
    step = start(y_step(late_sum2, late_y, LATE))
    arrive(early_step)
    early_step = start(x_back(early_ref, EARLY))
    arrive(step)
    late_sum3[...] = late_sum2[pl.ds(pl.multiple_of(y * 8, 8), 8), :] + late_y[0] + late_y[1] + late_y[2]
    late_z[z] = late_sum3[...]
    step = start(z_step(late_sum3, late_z, LATE))
    start(link(1))
    link_arrive(0)
    start(relay(0))
    arrive(step)
    late_ref[c, x, y] = late_z[0] + late_z[1] + late_z[2] + late_z[3]
    step = start(y_back(late_ref, LATE))
    arrive(early_step)
    early_step = start(core_back(early_ref, EARLY))
    arrive(step)
    step = start(x_back(late_ref, LATE))
    arrive(early_step)
    relay_arrive(0)
    arrive(step)
    step = start(core_back(late_ref, LATE))
    link_arrive(1)
    start(relay(1))
    arrive(step)
    relay_arrive(1)
    send(vec_ref, rest_ref.at[0], OWN, partner).wait_recv()
    for copy in started:
        copy.wait_send()


def exchange(vectors):
    rows, width = vectors.shape
    early = jax.ShapeDtypeStruct((2, 4, 4, 2, 8, 256), F32)
    late = jax.ShapeDtypeStruct((2, 4, 4, 8, 256), F32)
    rest = jax.ShapeDtypeStruct((3, rows, width), BF16)
    sums = [
        pltpu.VMEM((256, 256), F32), pltpu.VMEM((128, 256), F32), pltpu.VMEM((3, 32, 256), F32),
        pltpu.VMEM((3, 8, 256), F32), pltpu.VMEM((4, 8, 256), F32),
        pltpu.VMEM((128, 256), F32), pltpu.VMEM((32, 256), F32), pltpu.VMEM((8, 256), F32),
    ]
    return pl.pallas_call(
        exchange_kernel,
        out_shape=(early, late, rest),
        in_specs=[ANY],
        out_specs=(VMEM, VMEM, ANY),
        scratch_shapes=[
            pltpu.VMEM((2, rows // 2, width), BF16), pltpu.VMEM((4, rows // 4, width), BF16),
            *sums, *sums,
            pltpu.SemaphoreType.DMA, pltpu.SemaphoreType.DMA((SEMS,)), pltpu.SemaphoreType.DMA((SEMS,)),
        ],
        compiler_params=pltpu.CompilerParams(
            collective_id=0, has_side_effects=True, vmem_limit_bytes=24 * 2**20
        ),
        name="exchange",
    )(vectors)


def split(value):
    high = value.astype(BF16)
    return high, (value - high.astype(F32)).astype(BF16)


def product(left, right):
    (lh, ll), (rh, rl) = left, right
    dot = functools.partial(jnp.dot, preferred_element_type=F32)
    return dot(lh, rh) + (dot(lh, rl) + dot(ll, rh))


def finish_kernel(
    total_rows, active_ref, early_ref, late_ref, vec_ref, rest_ref, out_ref,
    matrix, factor, own, rest, result, in_sem, out_sem,
):
    s = lax.axis_index("state")
    zh, c = s // 2, s % 2
    rows = own.shape[0]
    loads = [pltpu.make_async_copy(vec_ref, own, in_sem.at[0])]
    loads += [pltpu.make_async_copy(rest_ref.at[k], rest.at[k], in_sem.at[1 + k]) for k in range(3)]
    for load in loads:
        load.start()

    def flags(shape, axis):
        state = lax.broadcasted_iota(jnp.int32, shape, axis) // VECS
        flag = jnp.zeros(shape, jnp.int32)
        for k in range(8):
            flag = jnp.where(state == k, active_ref[k], flag)
        return flag

    cols = matrix.shape[0]
    cross = late_ref[...].reshape(256, 256)
    matrix[0:256, 0:256] = early_ref[:, :, :, 0].reshape(256, 256)
    matrix[256:512, 256:512] = early_ref[:, :, :, 1].reshape(256, 256)
    matrix[0:256, 256:512] = cross
    matrix[256:512, 0:256] = cross.T
    row_flag, col_flag = flags((cols, 1), 0), flags((1, cols), 1)
    eye = lax.broadcasted_iota(jnp.int32, (cols, cols), 0) == lax.broadcasted_iota(jnp.int32, (cols, cols), 1)
    gram_matrix = jnp.where(row_flag * col_flag == 1, matrix[...], 0.0)
    gram_matrix = gram_matrix + jnp.where(eye & (row_flag == 0), total_rows, 0.0)
    frob_norm = jnp.sqrt(jnp.sum(gram_matrix * gram_matrix, keepdims=True))
    current = gram_matrix / frob_norm

    panel_eye = lax.broadcasted_iota(jnp.int32, (cols, 128), 0) == lax.broadcasted_iota(jnp.int32, (cols, 128), 1) + s * 128

    def advance(parts, current):
        first = 1.5 * current - 0.5 * product(parts, parts)
        return 1.5 * first - 0.5 * product(split(first), parts)

    matrix[...] = current
    column = matrix[:, pl.ds(pl.multiple_of(s * 128, 128), 128)]
    panel = jnp.where(panel_eye, 1.5, 0.0) - 0.5 * column
    parts = split(current)
    for step in range(2):
        current = advance(parts, current)
        parts = split(current)
        panel = 1.5 * panel - 0.5 * product(parts, split(panel))
    current = advance(parts, current)
    parts = split(current)
    moved = product(parts, split(panel))
    panel = 1.5 * panel - 0.5 * moved
    last = product(parts, split(panel))
    last = 1.5 * last - 0.5 * product(parts, split(last))
    last = 1.5 * last - 0.5 * product(parts, split(last))
    panel = 1.5 * panel - 0.5 * last
    panel = (panel * jnp.sqrt(total_rows / frob_norm)).astype(BF16)
    factor[...] = jnp.where(row_flag == 1, panel.astype(F32), 0.0)

    def factor_of(state):
        return factor[pl.ds(pl.multiple_of(state * 128, 128), 128), :].astype(BF16)

    near = jnp.concatenate([factor_of(s), factor_of(s + 1 - 2 * c)], axis=0)
    far = jnp.concatenate([factor_of(2 - 2 * zh), factor_of(3 - 2 * zh)], axis=0)
    keep = jnp.zeros((1, 128), jnp.int32)
    lane_state = lax.broadcasted_iota(jnp.int32, (1, 128), 1) // VECS + s * 2
    for k in range(8):
        keep = jnp.where(lane_state == k, active_ref[k], keep)
    for load in loads:
        load.wait()
    chunk = 512
    for k in range(rows // chunk):
        block = pl.ds(k * chunk, chunk)
        left = jnp.concatenate([own[block], rest[0, block]], axis=1)
        right = jnp.concatenate([rest[1, block], rest[2, block]], axis=1)
        value = jnp.dot(left, near, preferred_element_type=F32) + jnp.dot(right, far, preferred_element_type=F32)
        result[block] = jnp.where(keep == 1, value, own[block].astype(F32)).astype(BF16)
        pltpu.make_async_copy(result.at[block], out_ref.at[block], out_sem.at[k]).start()
    for k in range(rows // chunk):
        block = pl.ds(k * chunk, chunk)
        pltpu.make_async_copy(result.at[block], out_ref.at[block], out_sem.at[k]).wait()


def finish(total_rows, active, early, late, vectors, rest):
    rows, width = vectors.shape
    return pl.pallas_call(
        functools.partial(finish_kernel, total_rows),
        out_shape=jax.ShapeDtypeStruct((rows, width), BF16),
        in_specs=[pl.BlockSpec(memory_space=pltpu.SMEM), VMEM, VMEM, ANY, ANY],
        out_specs=ANY,
        scratch_shapes=[
            pltpu.VMEM((512, 512), F32), pltpu.VMEM((512, 128), F32),
            pltpu.VMEM((rows, width), BF16), pltpu.VMEM((3, rows, width), BF16), pltpu.VMEM((rows, width), BF16),
            pltpu.SemaphoreType.DMA((4,)), pltpu.SemaphoreType.DMA((8,)),
        ],
        compiler_params=pltpu.CompilerParams(vmem_limit_bytes=40 * 2**20),
        name="finish",
    )(active, early, late, vectors, rest)


def shards(vectors, active):
    total_rows = float(vectors.shape[0] * lax.axis_size("row"))
    early, late, rest = exchange(vectors)
    return finish(total_rows, active, early, late, vectors, rest)


def solution(mesh):
    in_specs = (P("row", "state"), P())
    out_specs = P("row", "state")
    return jax.shard_map(shards, mesh=mesh, in_specs=in_specs, out_specs=out_specs, check_vma=False)
```

```python
import functools

import jax
import jax.numpy as jnp
from jax import lax
from jax.experimental import pallas as pl
from jax.experimental.pallas import tpu as pltpu
from jax.sharding import PartitionSpec as P

VECS = 64
MESH = pl.DeviceIdType.MESH
F32 = jnp.float32
BF16 = jnp.bfloat16
ANY = pl.BlockSpec(memory_space=pl.ANY)
VMEM = pl.BlockSpec(memory_space=pltpu.VMEM)

HALF, QUARTER, OWN, LINK, RELAY, CORE, XDIM, YDIM, ZDIM, YBACK, XBACK, CBACK = 0, 1, 5, 6, 10, 14, 15, 18, 21, 24, 27, 30
LCORE, LOUT, LBACK, LCBACK, SEMS = 31, 32, 33, 34, 35
OFFSETS = [(a, b, d) for a in range(4) for b in range(4) for d in range(4)]


def hops(offset):
    return sum(min(v, 4 - v) for v in offset)


def gram(left, right):
    return lax.dot_general(left, right, (((0,), (0,)), ((), ())), preferred_element_type=F32)


def exchange_kernel(
    vec_ref, active_hbm, early_ref, late_ref, all_ref, flag_ref,
    active, half, quart, early_part, early_core, early_x, early_y, early_z, early_sum1, early_sum2, early_sum3,
    late_part, late_core, late_sum, late_got, mask, local_sem, send_sem, recv_sem,
):
    s, r = lax.axis_index("state"), lax.axis_index("row")
    zh, c = s // 2, s % 2
    zl, x, y = r // 16, (r // 4) % 4, r % 4
    z = zh * 2 + zl
    other_r = r + 16 * (1 - 2 * zl)
    near = s + 1 - 2 * c
    partner = (near, r)
    far = 2 - 2 * zh
    rows = vec_ref.shape[0]
    half_rows, quart_rows = rows // 2, rows // 4

    def device(offset):
        to_x, to_y, to_z = [(at + step) % 4 for at, step in zip((x, y, z), offset)]
        return ((to_z // 2) * 2 + c, (to_z % 2) * 16 + to_x * 4 + to_y)

    def x_peer(d):
        return device((d, 0, 0))

    def y_peer(d):
        return device((0, d, 0))

    def z_peer(d):
        return device((0, 0, d))

    def send(src, dst, sem, to, recv=None):
        return pltpu.make_async_remote_copy(
            src_ref=src, dst_ref=dst, send_sem=send_sem.at[sem],
            recv_sem=recv_sem.at[sem if recv is None else recv],
            device_id=to, device_id_type=MESH,
        )

    started = []

    def start(copies):
        for copy in copies:
            copy.start()
        started.extend(copies)
        return copies

    def arrive(copies):
        for copy in copies:
            copy.wait_recv()

    mine = pltpu.make_async_copy(vec_ref.at[pl.ds(c * half_rows, half_rows)], half.at[c], local_sem.at[0])
    mine.start()
    flag_copy = pltpu.make_async_copy(active_hbm, active, local_sem.at[1])
    flag_copy.start()
    own = pltpu.make_async_copy(vec_ref, all_ref.at[s], local_sem.at[2])
    own.start()

    barrier = pltpu.get_barrier_semaphore()
    peers = [partner] + [(t, other_r) for t in range(4)] + [z_peer(2)]
    peers += [x_peer(d) for d in (1, 2, 3)] + [y_peer(d) for d in (1, 2, 3)]
    for peer in peers:
        pl.semaphore_signal(barrier, inc=1, device_id=peer, device_id_type=MESH)
    pl.semaphore_wait(barrier, len(peers))

    halves = start([send(vec_ref.at[pl.ds((1 - c) * half_rows, half_rows)], half.at[c], HALF, partner)])
    start([
        send(vec_ref.at[pl.ds(t * quart_rows, quart_rows)], quart.at[s], QUARTER + t, (t, other_r), recv=QUARTER + s)
        for t in range(4)
    ])

    flag_copy.wait()

    def flags(shape, axis, first):
        state = lax.broadcasted_iota(jnp.int32, shape, axis) // VECS + first
        flag = jnp.zeros(shape, F32)
        for k in range(8):
            flag = jnp.where(state == k, active[k].astype(F32), flag)
        return flag

    flag_ref[...] = flags(flag_ref.shape, 1, 0)
    block = (256, 256)
    mask[...] = flags(block, 0, 0) * flags(block, 1, 4)
    early_mask = flags(block, 0, zh * 4) * flags(block, 1, zh * 4)

    mine.wait()
    arrive(halves)
    both = jnp.concatenate([half[0], half[1]], axis=1)
    early_part[...] = jnp.where(early_mask == 1.0, gram(both, both), 0.0)
    step = start([send(early_part.at[pl.ds((1 - c) * 128, 128)], early_core, CORE, partner)])
    arrive(step)
    early_sum1[...] = early_part[pl.ds(pl.multiple_of(c * 128, 128), 128), :] + early_core[...]
    step = start([
        send(early_sum1.at[pl.ds(((x + d) % 4) * 32, 32)], early_x.at[d - 1], XDIM + d - 1, x_peer(d)) for d in (1, 2, 3)
    ])
    start([send(vec_ref, all_ref.at[s], OWN, partner)])
    arrive(step)
    early_sum2[...] = early_sum1[pl.ds(pl.multiple_of(x * 32, 32), 32), :] + early_x[0] + early_x[1] + early_x[2]
    step = start([
        send(early_sum2.at[pl.ds(((y + d) % 4) * 8, 8)], early_y.at[d - 1], YDIM + d - 1, y_peer(d)) for d in (1, 2, 3)
    ])
    arrive(step)
    early_sum3[...] = early_sum2[pl.ds(pl.multiple_of(y * 8, 8), 8), :] + early_y[0] + early_y[1] + early_y[2]
    early_z[z] = early_sum3[...]
    early_step = start([send(early_sum3, early_z.at[z], ZDIM + d - 1, z_peer(d)) for d in (1, 2, 3)])

    for t in range(4):
        send(vec_ref.at[pl.ds(0, quart_rows)], quart.at[t], QUARTER + t, (t, other_r)).wait_recv()
    left = jnp.concatenate([quart[0], quart[1]], axis=1)
    right = jnp.concatenate([quart[2], quart[3]], axis=1)
    late_part[...] = jnp.where(mask[...] == 1.0, gram(left, right), 0.0)
    step = start([send(late_part.at[pl.ds((1 - c) * 128, 128)], late_core, LCORE, partner)])

    def link(part):
        return [
            send(
                quart.at[2 - 2 * to + part],
                all_ref.at[2 - 2 * to + part, pl.ds(s * quart_rows, quart_rows)],
                LINK + part * 2 + to,
                (to * 2 + c, other_r),
                recv=LINK + part * 2 + zh,
            )
            for to in (0, 1)
        ]

    def relay_copies(part, core):
        blocks = [all_ref.at[far + part, pl.ds((frm * 2 + core) * quart_rows, quart_rows)] for frm in (0, 1)]
        return [send(block, block, RELAY + part * 2 + frm, partner) for frm, block in enumerate(blocks)]

    def link_arrive(part):
        for frm in (0, 1):
            send(
                quart.at[0], all_ref.at[far + part, pl.ds((frm * 2 + c) * quart_rows, quart_rows)],
                LINK + part * 2 + frm, partner,
            ).wait_recv()

    arrive(step)
    total = late_part[pl.ds(pl.multiple_of(c * 128, 128), 128), :] + late_core[...]
    for k in (0, 1):
        late_sum[:, k] = total[:, k * 128:(k + 1) * 128].reshape(16, 8, 128)
    odd = (x + y + z + c) % 2
    place = x * 16 + y * 4 + z
    outward = sorted([(a, b, d) for a in range(4) for b in range(4) for d in (0, 2)], key=hops, reverse=True)

    def scatter(offset):
        a, b, d = offset
        d = d + (a + b + odd) % 2
        to_x, to_y, to_z = (x + a) % 4, (y + b) % 4, (z + d) % 4
        send(
            late_sum.at[to_x * 4 + to_y, to_z // 2], late_got.at[place], LOUT, device((a, b, d))
        ).start()

    for offset in outward:
        if offset == (0, 0, 0):
            pl.when(odd == 1)(functools.partial(scatter, offset))
        else:
            scatter(offset)
    start(link(0))
    arrive(early_step)
    early_ref[c, x, y, 0] = early_z[0] + early_z[1]
    early_ref[c, x, y, 1] = early_z[2] + early_z[3]
    early_step = start([
        send(early_ref.at[c, x, y], early_ref.at[c, x, y], YBACK + d - 1, y_peer(d)) for d in (1, 2, 3)
    ])
    arrive(early_step)

    here = (c, x * 4 + y, z // 2)

    @pl.when(odd == 0)
    def _():
        late_got[place] = late_sum[x * 4 + y, z // 2]
        whole = late_got.at[pl.ds(0, 63)]
        send(whole, whole, LOUT, partner).wait_recv()
        late_ref[here] = jnp.sum(late_got[...], axis=0)
        for offset in sorted(OFFSETS[1:], key=hops, reverse=True):
            send(late_ref.at[here], late_ref.at[here], LBACK, device(offset)).start()

    early_step = start([send(early_ref.at[c, x], early_ref.at[c, x], XBACK + d - 1, x_peer(d)) for d in (1, 2, 3)])
    start(link(1))
    link_arrive(0)
    start(relay_copies(0, c))
    arrive(early_step)
    early_step = start([send(early_ref.at[c], early_ref.at[c], CBACK, partner)])

    @pl.when(odd == 0)
    def _():
        gathered = late_got.at[pl.ds(0, 31)]
        send(gathered, gathered, LBACK, partner).wait_recv()

    @pl.when(odd == 1)
    def _():
        gathered = late_got.at[pl.ds(0, 32)]
        send(gathered, gathered, LBACK, partner).wait_recv()

    step = start([send(late_ref.at[c], late_ref.at[c], LCBACK, partner)])
    link_arrive(1)
    start(relay_copies(1, c))
    arrive(early_step)
    arrive(step)
    arrive(relay_copies(0, 1 - c))
    arrive(relay_copies(1, 1 - c))
    send(vec_ref, all_ref.at[near], OWN, partner).wait_recv()
    own.wait()

    @pl.when(odd == 0)
    def _():
        out, back = late_got.at[pl.ds(0, 31)], late_got.at[pl.ds(0, 63)]
        send(out, out, LOUT, partner).wait_send()
        send(back, back, LBACK, partner).wait_send()

    @pl.when(odd == 1)
    def _():
        out = late_got.at[pl.ds(0, 32)]
        send(out, out, LOUT, partner).wait_send()

    for copy in started:
        copy.wait_send()


def exchange(vectors, active):
    rows, width = vectors.shape
    hbm = pl.BlockSpec(memory_space=pltpu.HBM)
    return pl.pallas_call(
        exchange_kernel,
        out_shape=(
            jax.ShapeDtypeStruct((2, 4, 4, 2, 8, 256), F32),
            jax.ShapeDtypeStruct((2, 16, 2, 8, 128), F32),
            jax.ShapeDtypeStruct((4, rows, width), BF16),
            jax.ShapeDtypeStruct((8, 512), F32),
        ),
        in_specs=[hbm, hbm],
        out_specs=(VMEM, VMEM, VMEM, VMEM),
        scratch_shapes=[
            pltpu.SMEM((8,), jnp.int32),
            pltpu.VMEM((2, rows // 2, width), BF16), pltpu.VMEM((4, rows // 4, width), BF16),
            pltpu.VMEM((256, 256), F32), pltpu.VMEM((128, 256), F32), pltpu.VMEM((3, 32, 256), F32),
            pltpu.VMEM((3, 8, 256), F32), pltpu.VMEM((4, 8, 256), F32),
            pltpu.VMEM((128, 256), F32), pltpu.VMEM((32, 256), F32), pltpu.VMEM((8, 256), F32),
            pltpu.VMEM((256, 256), F32), pltpu.VMEM((128, 256), F32), pltpu.VMEM((16, 2, 8, 128), F32),
            pltpu.VMEM((64, 8, 128), F32), pltpu.VMEM((256, 256), F32),
            pltpu.SemaphoreType.DMA((3,)), pltpu.SemaphoreType.DMA((SEMS,)), pltpu.SemaphoreType.DMA((SEMS,)),
        ],
        compiler_params=pltpu.CompilerParams(
            collective_id=0, has_side_effects=True, vmem_limit_bytes=24 * 2**20
        ),
        name="exchange",
    )(*[pltpu.with_memory_space_constraint(v, pltpu.HBM) for v in (vectors, active)])


def split(value):
    high = value.astype(BF16)
    return high, (value - high.astype(F32)).astype(BF16)


def product(left, right):
    (lh, ll), (rh, rl) = left, right
    dot = functools.partial(jnp.dot, preferred_element_type=F32)
    return dot(lh, rh) + (dot(lh, rl) + dot(ll, rh))


def finish_kernel(
    total_rows, early_ref, late_ref, all_ref, flag_ref, out_ref, matrix, factor, result, out_sem,
):
    s = lax.axis_index("state")
    rows = all_ref.shape[1]
    cols = matrix.shape[0]
    cross = jnp.concatenate([late_ref[:, :, k].reshape(256, 128) for k in (0, 1)], axis=1)
    matrix[0:256, 0:256] = early_ref[:, :, :, 0].reshape(256, 256)
    matrix[256:512, 256:512] = early_ref[:, :, :, 1].reshape(256, 256)
    matrix[0:256, 256:512] = cross
    matrix[256:512, 0:256] = cross.T
    eye = lax.broadcasted_iota(jnp.int32, (cols, cols), 0) == lax.broadcasted_iota(jnp.int32, (cols, cols), 1)
    gram_matrix = matrix[...] + jnp.where(eye & (flag_ref[0:1, :] == 0.0), total_rows, 0.0)
    frob_norm = jnp.sqrt(jnp.sum(gram_matrix * gram_matrix, keepdims=True))
    current = gram_matrix / frob_norm

    panel_eye = lax.broadcasted_iota(jnp.int32, (cols, 128), 0) == lax.broadcasted_iota(jnp.int32, (cols, 128), 1) + s * 128

    def advance(parts, current):
        first = 1.5 * current - 0.5 * product(parts, parts)
        return 1.5 * first - 0.5 * product(split(first), parts)

    matrix[...] = current
    column = matrix[:, pl.ds(pl.multiple_of(s * 128, 128), 128)]
    panel = jnp.where(panel_eye, 1.5, 0.0) - 0.5 * column
    parts = split(current)
    for step in range(2):
        current = advance(parts, current)
        parts = split(current)
        panel = 1.5 * panel - 0.5 * product(parts, split(panel))
    current = advance(parts, current)
    parts = split(current)
    moved = product(parts, split(panel))
    panel = 1.5 * panel - 0.5 * moved
    last = product(parts, split(panel))
    last = 1.5 * last - 0.5 * product(parts, split(last))
    last = 1.5 * last - 0.5 * product(parts, split(last))
    panel = 1.5 * panel - 0.5 * last
    factor[...] = panel * jnp.sqrt(total_rows / frob_norm)

    def factor_of(state):
        return factor[pl.ds(pl.multiple_of(state * 128, 128), 128), :].astype(BF16)

    near = jnp.concatenate([factor_of(0), factor_of(1)], axis=0)
    far = jnp.concatenate([factor_of(2), factor_of(3)], axis=0)
    keep = flag_ref[0:1, pl.ds(pl.multiple_of(s * 128, 128), 128)]
    chunk = 512
    for k in range(rows // chunk):
        block = pl.ds(k * chunk, chunk)
        left = jnp.concatenate([all_ref[0, block], all_ref[1, block]], axis=1)
        right = jnp.concatenate([all_ref[2, block], all_ref[3, block]], axis=1)
        value = jnp.dot(left, near, preferred_element_type=F32) + jnp.dot(right, far, preferred_element_type=F32)
        result[block] = jnp.where(keep == 1.0, value, all_ref[s, block].astype(F32)).astype(BF16)
        pltpu.make_async_copy(result.at[block], out_ref.at[block], out_sem.at[k]).start()
    for k in range(rows // chunk):
        block = pl.ds(k * chunk, chunk)
        pltpu.make_async_copy(result.at[block], out_ref.at[block], out_sem.at[k]).wait()


def finish(total_rows, early, late, everything, flag):
    rows, width = everything.shape[1:]
    return pl.pallas_call(
        functools.partial(finish_kernel, total_rows),
        out_shape=jax.ShapeDtypeStruct((rows, width), BF16),
        in_specs=[VMEM] * 4,
        out_specs=ANY,
        scratch_shapes=[
            pltpu.VMEM((512, 512), F32), pltpu.VMEM((512, 128), F32), pltpu.VMEM((rows, width), BF16),
            pltpu.SemaphoreType.DMA((8,)),
        ],
        compiler_params=pltpu.CompilerParams(vmem_limit_bytes=40 * 2**20),
        name="finish",
    )(early, late, everything, flag)


def shards(vectors, active):
    total_rows = float(vectors.shape[0] * lax.axis_size("row"))
    return finish(total_rows, *exchange(vectors, active))


def solution(mesh):
    in_specs = (P("row", "state"), P())
    out_specs = P("row", "state")
    return jax.shard_map(shards, mesh=mesh, in_specs=in_specs, out_specs=out_specs, check_vma=False)
```

```python
import functools

import jax
import jax.numpy as jnp
from jax import lax
from jax.experimental import pallas as pl
from jax.experimental.pallas import tpu as pltpu
from jax.sharding import PartitionSpec as P

VECS = 64
MESH = pl.DeviceIdType.MESH
F32 = jnp.float32
BF16 = jnp.bfloat16
ANY = pl.BlockSpec(memory_space=pl.ANY)
VMEM = pl.BlockSpec(memory_space=pltpu.VMEM)

HALF, QUARTER, OWN, LINK, RELAY, CORE, XDIM, YDIM, ZDIM, YBACK, XBACK, CBACK = 0, 1, 5, 6, 10, 14, 15, 18, 21, 24, 27, 30
LCORE, LOUT, LBACK, LCBACK, SEMS = 31, 32, 33, 34, 35
OFFSETS = [(a, b, d) for a in range(4) for b in range(4) for d in range(4)]


def hops(offset):
    return sum(min(v, 4 - v) for v in offset)


def gram(left, right):
    return lax.dot_general(left, right, (((0,), (0,)), ((), ())), preferred_element_type=F32)


def exchange_kernel(
    vec_ref, active_hbm, early_ref, late_ref, all_ref, flag_ref,
    active, half, quart, early_part, early_core, early_x, early_y, early_z, early_sum1, early_sum2, early_sum3,
    late_part, late_core, late_sum, late_got, mask, local_sem, send_sem, recv_sem,
):
    s, r = lax.axis_index("state"), lax.axis_index("row")
    zh, c = s // 2, s % 2
    zl, x, y = r // 16, (r // 4) % 4, r % 4
    z = zh * 2 + zl
    other_r = r + 16 * (1 - 2 * zl)
    near = s + 1 - 2 * c
    partner = (near, r)
    far = 2 - 2 * zh
    rows = vec_ref.shape[0]
    half_rows, quart_rows = rows // 2, rows // 4

    def device(offset):
        to_x, to_y, to_z = [(at + step) % 4 for at, step in zip((x, y, z), offset)]
        return ((to_z // 2) * 2 + c, (to_z % 2) * 16 + to_x * 4 + to_y)

    def x_peer(d):
        return device((d, 0, 0))

    def y_peer(d):
        return device((0, d, 0))

    def z_peer(d):
        return device((0, 0, d))

    def send(src, dst, sem, to, recv=None):
        return pltpu.make_async_remote_copy(
            src_ref=src, dst_ref=dst, send_sem=send_sem.at[sem],
            recv_sem=recv_sem.at[sem if recv is None else recv],
            device_id=to, device_id_type=MESH,
        )

    started = []

    def start(copies):
        for copy in copies:
            copy.start()
        started.extend(copies)
        return copies

    def arrive(copies):
        for copy in copies:
            copy.wait_recv()

    mine = pltpu.make_async_copy(vec_ref.at[pl.ds(c * half_rows, half_rows)], half.at[c], local_sem.at[0])
    mine.start()
    flag_copy = pltpu.make_async_copy(active_hbm, active, local_sem.at[1])
    flag_copy.start()
    own = pltpu.make_async_copy(vec_ref, all_ref.at[s], local_sem.at[2])
    own.start()

    barrier = pltpu.get_barrier_semaphore()
    peers = [partner] + [(t, other_r) for t in range(4)] + [z_peer(2)]
    peers += [x_peer(d) for d in (1, 2, 3)] + [y_peer(d) for d in (1, 2, 3)]
    for peer in peers:
        pl.semaphore_signal(barrier, inc=1, device_id=peer, device_id_type=MESH)
    pl.semaphore_wait(barrier, len(peers))

    halves = start([send(vec_ref.at[pl.ds((1 - c) * half_rows, half_rows)], half.at[c], HALF, partner)])
    start([
        send(vec_ref.at[pl.ds(t * quart_rows, quart_rows)], quart.at[s], QUARTER + t, (t, other_r), recv=QUARTER + s)
        for t in range(4)
    ])

    flag_copy.wait()

    def flags(shape, axis, first):
        state = lax.broadcasted_iota(jnp.int32, shape, axis) // VECS + first
        flag = jnp.zeros(shape, F32)
        for k in range(8):
            flag = jnp.where(state == k, active[k].astype(F32), flag)
        return flag

    flag_ref[...] = flags(flag_ref.shape, 1, 0)
    block = (256, 256)
    mask[...] = flags(block, 0, 0) * flags(block, 1, 4)
    early_mask = flags(block, 0, zh * 4) * flags(block, 1, zh * 4)

    mine.wait()
    arrive(halves)
    both = jnp.concatenate([half[0], half[1]], axis=1)
    early_part[...] = jnp.where(early_mask == 1.0, gram(both, both), 0.0)
    step = start([send(early_part.at[pl.ds((1 - c) * 128, 128)], early_core, CORE, partner)])
    arrive(step)
    early_sum1[...] = early_part[pl.ds(pl.multiple_of(c * 128, 128), 128), :] + early_core[...]
    step = start([
        send(early_sum1.at[pl.ds(((x + d) % 4) * 32, 32)], early_x.at[d - 1], XDIM + d - 1, x_peer(d)) for d in (1, 2, 3)
    ])
    start([send(vec_ref, all_ref.at[s], OWN, partner)])
    arrive(step)
    early_sum2[...] = early_sum1[pl.ds(pl.multiple_of(x * 32, 32), 32), :] + early_x[0] + early_x[1] + early_x[2]
    step = start([
        send(early_sum2.at[pl.ds(((y + d) % 4) * 8, 8)], early_y.at[d - 1], YDIM + d - 1, y_peer(d)) for d in (1, 2, 3)
    ])
    arrive(step)
    early_sum3[...] = early_sum2[pl.ds(pl.multiple_of(y * 8, 8), 8), :] + early_y[0] + early_y[1] + early_y[2]
    early_z[z] = early_sum3[...]
    early_step = start([send(early_sum3, early_z.at[z], ZDIM + d - 1, z_peer(d)) for d in (1, 2, 3)])

    for t in range(4):
        send(vec_ref.at[pl.ds(0, quart_rows)], quart.at[t], QUARTER + t, (t, other_r)).wait_recv()
    left = jnp.concatenate([quart[0], quart[1]], axis=1)
    right = jnp.concatenate([quart[2], quart[3]], axis=1)
    late_part[...] = jnp.where(mask[...] == 1.0, gram(left, right), 0.0)
    step = start([send(late_part.at[pl.ds((1 - c) * 128, 128)], late_core, LCORE, partner)])

    def link(part):
        return [
            send(
                quart.at[2 - 2 * to + part],
                all_ref.at[2 - 2 * to + part, pl.ds(s * quart_rows, quart_rows)],
                LINK + part * 2 + to,
                (to * 2 + c, other_r),
                recv=LINK + part * 2 + zh,
            )
            for to in (0, 1)
        ]

    def relay_copies(part, core):
        blocks = [all_ref.at[far + part, pl.ds((frm * 2 + core) * quart_rows, quart_rows)] for frm in (0, 1)]
        return [send(block, block, RELAY + part * 2 + frm, partner) for frm, block in enumerate(blocks)]

    def link_arrive(part):
        for frm in (0, 1):
            send(
                quart.at[0], all_ref.at[far + part, pl.ds((frm * 2 + c) * quart_rows, quart_rows)],
                LINK + part * 2 + frm, partner,
            ).wait_recv()

    arrive(step)
    total = late_part[pl.ds(pl.multiple_of(c * 128, 128), 128), :] + late_core[...]
    for k in (0, 1):
        late_sum[:, k] = total[:, k * 128:(k + 1) * 128].reshape(16, 8, 128)
    odd = (x + y + z + c) % 2
    place = x * 16 + y * 4 + z
    outward = sorted([(a, b, d) for a in range(4) for b in range(4) for d in (0, 2)], key=hops, reverse=True)

    def scatter(offset):
        a, b, d = offset
        d = d + (a + b + odd) % 2
        to_x, to_y, to_z = (x + a) % 4, (y + b) % 4, (z + d) % 4
        send(
            late_sum.at[to_x * 4 + to_y, to_z // 2], late_got.at[place], LOUT, device((a, b, d))
        ).start()

    for offset in outward:
        if offset == (0, 0, 0):
            pl.when(odd == 1)(functools.partial(scatter, offset))
        else:
            scatter(offset)
    start(link(0))
    arrive(early_step)
    early_ref[c, x, y, 0] = early_z[0] + early_z[1]
    early_ref[c, x, y, 1] = early_z[2] + early_z[3]
    early_step = start([
        send(early_ref.at[c, x, y], early_ref.at[c, x, y], YBACK + d - 1, y_peer(d)) for d in (1, 2, 3)
    ])
    arrive(early_step)

    here = (c, x * 4 + y, z // 2)

    @pl.when(odd == 0)
    def _():
        late_got[place] = late_sum[x * 4 + y, z // 2]
        whole = late_got.at[pl.ds(0, 63)]
        send(whole, whole, LOUT, partner).wait_recv()
        late_ref[here] = jnp.sum(late_got[...], axis=0)
        for offset in sorted(OFFSETS[1:], key=hops, reverse=True):
            send(late_ref.at[here], late_ref.at[here], LBACK, device(offset)).start()

    early_step = start([send(early_ref.at[c, x], early_ref.at[c, x], XBACK + d - 1, x_peer(d)) for d in (1, 2, 3)])
    start(link(1))
    link_arrive(0)
    start(relay_copies(0, c))
    arrive(early_step)
    early_step = start([send(early_ref.at[c], early_ref.at[c], CBACK, partner)])

    @pl.when(odd == 0)
    def _():
        gathered = late_got.at[pl.ds(0, 31)]
        send(gathered, gathered, LBACK, partner).wait_recv()

    @pl.when(odd == 1)
    def _():
        gathered = late_got.at[pl.ds(0, 32)]
        send(gathered, gathered, LBACK, partner).wait_recv()

    step = start([send(late_ref.at[c], late_ref.at[c], LCBACK, partner)])
    link_arrive(1)
    start(relay_copies(1, c))
    arrive(early_step)
    arrive(step)
    arrive(relay_copies(0, 1 - c))
    arrive(relay_copies(1, 1 - c))
    send(vec_ref, all_ref.at[near], OWN, partner).wait_recv()
    own.wait()

    @pl.when(odd == 0)
    def _():
        out, back = late_got.at[pl.ds(0, 31)], late_got.at[pl.ds(0, 63)]
        send(out, out, LOUT, partner).wait_send()
        send(back, back, LBACK, partner).wait_send()

    @pl.when(odd == 1)
    def _():
        out = late_got.at[pl.ds(0, 32)]
        send(out, out, LOUT, partner).wait_send()

    for copy in started:
        copy.wait_send()


def exchange(vectors, active):
    rows, width = vectors.shape
    hbm = pl.BlockSpec(memory_space=pltpu.HBM)
    return pl.pallas_call(
        exchange_kernel,
        out_shape=(
            jax.ShapeDtypeStruct((2, 4, 4, 2, 8, 256), F32),
            jax.ShapeDtypeStruct((2, 16, 2, 8, 128), F32),
            jax.ShapeDtypeStruct((4, rows, width), BF16),
            jax.ShapeDtypeStruct((8, 512), F32),
        ),
        in_specs=[hbm, hbm],
        out_specs=(VMEM, VMEM, VMEM, VMEM),
        scratch_shapes=[
            pltpu.SMEM((8,), jnp.int32),
            pltpu.VMEM((2, rows // 2, width), BF16), pltpu.VMEM((4, rows // 4, width), BF16),
            pltpu.VMEM((256, 256), F32), pltpu.VMEM((128, 256), F32), pltpu.VMEM((3, 32, 256), F32),
            pltpu.VMEM((3, 8, 256), F32), pltpu.VMEM((4, 8, 256), F32),
            pltpu.VMEM((128, 256), F32), pltpu.VMEM((32, 256), F32), pltpu.VMEM((8, 256), F32),
            pltpu.VMEM((256, 256), F32), pltpu.VMEM((128, 256), F32), pltpu.VMEM((16, 2, 8, 128), F32),
            pltpu.VMEM((64, 8, 128), F32), pltpu.VMEM((256, 256), F32),
            pltpu.SemaphoreType.DMA((3,)), pltpu.SemaphoreType.DMA((SEMS,)), pltpu.SemaphoreType.DMA((SEMS,)),
        ],
        compiler_params=pltpu.CompilerParams(
            collective_id=0, has_side_effects=True, vmem_limit_bytes=24 * 2**20
        ),
        name="exchange",
    )(*[pltpu.with_memory_space_constraint(v, pltpu.HBM) for v in (vectors, active)])


def split(value):
    high = value.astype(BF16)
    return high, (value - high.astype(F32)).astype(BF16)


def product(left, right):
    (lh, ll), (rh, rl) = left, right
    return jnp.dot(
        jnp.concatenate([ll, lh, lh], axis=1), jnp.concatenate([rh, rl, rh], axis=0), preferred_element_type=F32
    )


def mirrored(left, right, below=None):
    h = left[0].shape[0] // 2
    upper = [v[:h] for v in left]
    if below is not None:
        upper = [jnp.concatenate(pair, axis=0) for pair in zip(upper, below)]
    top = product(upper, right)
    low = product([v[h:] for v in left], [v[:, h:] for v in right])
    top, rest = top[:h], top[h:]
    return jnp.concatenate([top, jnp.concatenate([top[:, h:].T, low], axis=1)], axis=0), rest


def narrow(left, right):
    (lh, ll), (rh, rl) = left, right
    rows = lh.shape[0]
    both = jnp.dot(jnp.concatenate([lh, ll], axis=0), rh, preferred_element_type=F32)
    return both[:rows] + (both[rows:] + jnp.dot(lh, rl, preferred_element_type=F32))


def finish_kernel(
    total_rows, early_ref, late_ref, all_ref, flag_ref, out_ref, matrix, result, out_sem,
):
    s = lax.axis_index("state")
    rows = all_ref.shape[1]
    cols = matrix.shape[0]
    cross = jnp.concatenate([late_ref[:, :, k].reshape(256, 128) for k in (0, 1)], axis=1)
    matrix[0:256, 0:256] = early_ref[:, :, :, 0].reshape(256, 256)
    matrix[256:512, 256:512] = early_ref[:, :, :, 1].reshape(256, 256)
    matrix[0:256, 256:512] = cross
    matrix[256:512, 0:256] = cross.T
    eye = lax.broadcasted_iota(jnp.int32, (cols, cols), 0) == lax.broadcasted_iota(jnp.int32, (cols, cols), 1)
    gram_matrix = matrix[...] + jnp.where(eye & (flag_ref[0:1, :] == 0.0), total_rows, 0.0)
    frob_norm = jnp.sqrt(jnp.sum(gram_matrix * gram_matrix, keepdims=True))
    current = gram_matrix / frob_norm

    rows_of = pl.ds(pl.multiple_of(s * 128, 128), 128)
    panel_eye = lax.broadcasted_iota(jnp.int32, (128, cols), 0) + s * 128 == lax.broadcasted_iota(jnp.int32, (128, cols), 1)

    def advance(parts, current, panel):
        square, moved = mirrored(parts, parts, None if panel is None else split(panel))
        first = 1.5 * current - 0.5 * square
        current = 1.5 * first - 0.5 * mirrored(split(first), parts)[0]
        if panel is not None:
            panel = 1.5 * panel - 0.5 * moved
        return split(current), current, panel

    matrix[...] = current
    first_panel = jnp.where(panel_eye, 1.5, 0.0) - 0.5 * matrix[rows_of, :]
    parts, current, _ = advance(split(current), current, None)
    parts, current, panel = advance(parts, current, first_panel)
    parts, current, panel = advance(parts, current, panel)
    panel = 1.5 * panel - 0.5 * narrow(split(panel), parts)
    last = narrow(split(panel), parts)
    last = 1.5 * last - 0.5 * narrow(split(last), parts)
    last = 1.5 * last - 0.5 * narrow(split(last), parts)
    panel = 1.5 * panel - 0.5 * last
    factor = (panel * jnp.sqrt(total_rows / frob_norm)).astype(BF16)
    keep = flag_ref[0:1, pl.ds(pl.multiple_of(s * 128, 128), 128)]
    chunk = 512
    for k in range(rows // chunk):
        block = pl.ds(k * chunk, chunk)
        left = jnp.concatenate([all_ref[k4, block] for k4 in range(4)], axis=1)
        value = lax.dot_general(left, factor, (((1,), (1,)), ((), ())), preferred_element_type=F32)
        result[block] = jnp.where(keep == 1.0, value, all_ref[s, block].astype(F32)).astype(BF16)
        pltpu.make_async_copy(result.at[block], out_ref.at[block], out_sem.at[k]).start()
    for k in range(rows // chunk):
        block = pl.ds(k * chunk, chunk)
        pltpu.make_async_copy(result.at[block], out_ref.at[block], out_sem.at[k]).wait()


def finish(total_rows, early, late, everything, flag):
    rows, width = everything.shape[1:]
    return pl.pallas_call(
        functools.partial(finish_kernel, total_rows),
        out_shape=jax.ShapeDtypeStruct((rows, width), BF16),
        in_specs=[VMEM] * 4,
        out_specs=ANY,
        scratch_shapes=[
            pltpu.VMEM((512, 512), F32), pltpu.VMEM((rows, width), BF16),
            pltpu.SemaphoreType.DMA((8,)),
        ],
        compiler_params=pltpu.CompilerParams(vmem_limit_bytes=40 * 2**20),
        name="finish",
    )(early, late, everything, flag)


def shards(vectors, active):
    total_rows = float(vectors.shape[0] * lax.axis_size("row"))
    return finish(total_rows, *exchange(vectors, active))


def solution(mesh):
    in_specs = (P("row", "state"), P())
    out_specs = P("row", "state")
    return jax.shard_map(shards, mesh=mesh, in_specs=in_specs, out_specs=out_specs, check_vma=False)
```

```python
import functools

import jax
import jax.numpy as jnp
from jax import lax
from jax.experimental import pallas as pl
from jax.experimental.pallas import tpu as pltpu
from jax.sharding import PartitionSpec as P

VECS = 64
MESH = pl.DeviceIdType.MESH
F32 = jnp.float32
BF16 = jnp.bfloat16
ANY = pl.BlockSpec(memory_space=pl.ANY)
VMEM = pl.BlockSpec(memory_space=pltpu.VMEM)

HALF, QUARTER, OWN, CORE, XDIM, YDIM, ZDIM, YBACK, XBACK, CBACK = 0, 1, 5, 6, 7, 10, 13, 16, 19, 22
LCORE, LOUT, LBACK, LCBACK, LINK, RELAY, SEMS = 23, 24, 25, 26, 27, 43, 59
CHUNKS = 8
PLAN = ((0,), (1, 2, 3, 4), (5, 6, 7))
OFFSETS = [(a, b, d) for a in range(4) for b in range(4) for d in range(4)]


def hops(offset):
    return sum(min(v, 4 - v) for v in offset)


def gram(left, right):
    return lax.dot_general(left, right, (((0,), (0,)), ((), ())), preferred_element_type=F32)


def exchange_kernel(
    vec_ref, active_hbm, early_ref, late_ref, all_ref, flag_ref,
    active, half, quart, early_part, early_core, early_x, early_y, early_z, early_sum1, early_sum2, early_sum3,
    late_part, late_core, late_sum, late_got, mask, local_sem, send_sem, recv_sem,
):
    s, r = lax.axis_index("state"), lax.axis_index("row")
    zh, c = s // 2, s % 2
    zl, x, y = r // 16, (r // 4) % 4, r % 4
    z = zh * 2 + zl
    other_r = r + 16 * (1 - 2 * zl)
    near = s + 1 - 2 * c
    partner = (near, r)
    far = 2 - 2 * zh
    rows = vec_ref.shape[0]
    half_rows, quart_rows = rows // 2, rows // 4

    def device(offset):
        to_x, to_y, to_z = [(at + step) % 4 for at, step in zip((x, y, z), offset)]
        return ((to_z // 2) * 2 + c, (to_z % 2) * 16 + to_x * 4 + to_y)

    def x_peer(d):
        return device((d, 0, 0))

    def y_peer(d):
        return device((0, d, 0))

    def z_peer(d):
        return device((0, 0, d))

    def send(src, dst, sem, to, recv=None):
        return pltpu.make_async_remote_copy(
            src_ref=src, dst_ref=dst, send_sem=send_sem.at[sem],
            recv_sem=recv_sem.at[sem if recv is None else recv],
            device_id=to, device_id_type=MESH,
        )

    started = []

    def start(copies):
        for copy in copies:
            copy.start()
        started.extend(copies)
        return copies

    def arrive(copies):
        for copy in copies:
            copy.wait_recv()

    mine = pltpu.make_async_copy(vec_ref.at[pl.ds(c * half_rows, half_rows)], half.at[c], local_sem.at[0])
    mine.start()
    flag_copy = pltpu.make_async_copy(active_hbm, active, local_sem.at[1])
    flag_copy.start()
    own = pltpu.make_async_copy(vec_ref, all_ref.at[s], local_sem.at[2])
    own.start()

    barrier = pltpu.get_barrier_semaphore()
    peers = [partner] + [(t, other_r) for t in range(4)] + [z_peer(2)]
    peers += [x_peer(d) for d in (1, 2, 3)] + [y_peer(d) for d in (1, 2, 3)]
    for peer in peers:
        pl.semaphore_signal(barrier, inc=1, device_id=peer, device_id_type=MESH)
    pl.semaphore_wait(barrier, len(peers))

    halves = start([send(vec_ref.at[pl.ds((1 - c) * half_rows, half_rows)], half.at[c], HALF, partner)])
    start([
        send(vec_ref.at[pl.ds(t * quart_rows, quart_rows)], quart.at[s], QUARTER + t, (t, other_r), recv=QUARTER + s)
        for t in range(4)
    ])

    flag_copy.wait()

    def flags(shape, axis, first):
        state = lax.broadcasted_iota(jnp.int32, shape, axis) // VECS + first
        flag = jnp.zeros(shape, F32)
        for k in range(8):
            flag = jnp.where(state == k, active[k].astype(F32), flag)
        return flag

    flag_ref[...] = flags(flag_ref.shape, 1, 0)
    block = (256, 256)
    mask[...] = flags(block, 0, 0) * flags(block, 1, 4)
    early_mask = flags(block, 0, zh * 4) * flags(block, 1, zh * 4)

    mine.wait()
    arrive(halves)
    both = jnp.concatenate([half[0], half[1]], axis=1)
    early_part[...] = jnp.where(early_mask == 1.0, gram(both, both), 0.0)
    step = start([send(early_part.at[pl.ds((1 - c) * 128, 128)], early_core, CORE, partner)])
    arrive(step)
    early_sum1[...] = early_part[pl.ds(pl.multiple_of(c * 128, 128), 128), :] + early_core[...]
    step = start([
        send(early_sum1.at[pl.ds(((x + d) % 4) * 32, 32)], early_x.at[d - 1], XDIM + d - 1, x_peer(d)) for d in (1, 2, 3)
    ])
    start([send(vec_ref, all_ref.at[s], OWN, partner)])
    arrive(step)
    early_sum2[...] = early_sum1[pl.ds(pl.multiple_of(x * 32, 32), 32), :] + early_x[0] + early_x[1] + early_x[2]
    step = start([
        send(early_sum2.at[pl.ds(((y + d) % 4) * 8, 8)], early_y.at[d - 1], YDIM + d - 1, y_peer(d)) for d in (1, 2, 3)
    ])
    arrive(step)
    early_sum3[...] = early_sum2[pl.ds(pl.multiple_of(y * 8, 8), 8), :] + early_y[0] + early_y[1] + early_y[2]
    early_z[z] = early_sum3[...]

    chunk_rows = 2 * quart_rows // CHUNKS

    def chunk_at(chunk, core, frm):
        part, piece = chunk // (CHUNKS // 2), chunk % (CHUNKS // 2)
        return all_ref.at[far + part, pl.ds((frm * 2 + core) * quart_rows + piece * chunk_rows, chunk_rows)]

    def link(chunk):
        part, piece = chunk // (CHUNKS // 2), chunk % (CHUNKS // 2)
        return [
            send(
                quart.at[2 - 2 * to + part, pl.ds(piece * chunk_rows, chunk_rows)],
                all_ref.at[2 - 2 * to + part, pl.ds(s * quart_rows + piece * chunk_rows, chunk_rows)],
                LINK + chunk * 2 + to, (to * 2 + c, other_r), recv=LINK + chunk * 2 + zh,
            )
            for to in (0, 1)
        ]

    def relay_copies(chunk, core):
        blocks = [chunk_at(chunk, core, frm) for frm in (0, 1)]
        return [send(block, block, RELAY + chunk * 2 + frm, partner) for frm, block in enumerate(blocks)]

    def relay(chunk):
        for frm in (0, 1):
            block = chunk_at(chunk, c, frm)
            send(block, block, LINK + chunk * 2 + frm, partner).wait_recv()
        start(relay_copies(chunk, c))

    for t in range(4):
        send(vec_ref.at[pl.ds(0, quart_rows)], quart.at[t], QUARTER + t, (t, other_r)).wait_recv()
    early_step = start([send(early_sum3, early_z.at[z], ZDIM + d - 1, z_peer(d)) for d in (1, 2, 3)])
    for chunk in PLAN[0]:
        start(link(chunk))
    left = jnp.concatenate([quart[0], quart[1]], axis=1)
    right = jnp.concatenate([quart[2], quart[3]], axis=1)
    late_part[...] = jnp.where(mask[...] == 1.0, gram(left, right), 0.0)
    step = start([send(late_part.at[pl.ds((1 - c) * 128, 128)], late_core, LCORE, partner)])
    arrive(step)
    total = late_part[pl.ds(pl.multiple_of(c * 128, 128), 128), :] + late_core[...]
    for k in (0, 1):
        late_sum[:, k] = total[:, k * 128:(k + 1) * 128].reshape(16, 8, 128)
    odd = (x + y + z + c) % 2
    place = x * 16 + y * 4 + z
    outward = sorted([(a, b, d) for a in range(4) for b in range(4) for d in (0, 2)], key=hops, reverse=True)

    def scatter(offset):
        a, b, d = offset
        d = d + (a + b + odd) % 2
        to_x, to_y, to_z = (x + a) % 4, (y + b) % 4, (z + d) % 4
        send(
            late_sum.at[to_x * 4 + to_y, to_z // 2], late_got.at[place], LOUT, device((a, b, d))
        ).start()

    for offset in outward:
        if offset == (0, 0, 0):
            pl.when(odd == 1)(functools.partial(scatter, offset))
        else:
            scatter(offset)
    for chunk in PLAN[1]:
        start(link(chunk))
    arrive(early_step)
    early_ref[c, x, y, 0] = early_z[0] + early_z[1]
    early_ref[c, x, y, 1] = early_z[2] + early_z[3]
    early_step = start([
        send(early_ref.at[c, x, y], early_ref.at[c, x, y], YBACK + d - 1, y_peer(d)) for d in (1, 2, 3)
    ])
    for chunk in PLAN[0]:
        relay(chunk)

    here = (c, x * 4 + y, z // 2)

    @pl.when(odd == 0)
    def _():
        late_got[place] = late_sum[x * 4 + y, z // 2]
        whole = late_got.at[pl.ds(0, 63)]
        send(whole, whole, LOUT, partner).wait_recv()
        late_ref[here] = jnp.sum(late_got[...], axis=0)
        for offset in sorted(OFFSETS[1:], key=hops, reverse=True):
            send(late_ref.at[here], late_ref.at[here], LBACK, device(offset)).start()

    arrive(early_step)
    early_step = start([send(early_ref.at[c, x], early_ref.at[c, x], XBACK + d - 1, x_peer(d)) for d in (1, 2, 3)])
    for chunk in PLAN[2]:
        start(link(chunk))
    for chunk in PLAN[1]:
        relay(chunk)
    arrive(early_step)
    early_step = start([send(early_ref.at[c], early_ref.at[c], CBACK, partner)])

    @pl.when(odd == 0)
    def _():
        gathered = late_got.at[pl.ds(0, 31)]
        send(gathered, gathered, LBACK, partner).wait_recv()

    @pl.when(odd == 1)
    def _():
        gathered = late_got.at[pl.ds(0, 32)]
        send(gathered, gathered, LBACK, partner).wait_recv()

    step = start([send(late_ref.at[c], late_ref.at[c], LCBACK, partner)])
    for chunk in PLAN[2]:
        relay(chunk)
    arrive(early_step)
    arrive(step)
    for chunk in range(CHUNKS):
        arrive(relay_copies(chunk, 1 - c))
    send(vec_ref, all_ref.at[near], OWN, partner).wait_recv()
    own.wait()

    @pl.when(odd == 0)
    def _():
        out, back = late_got.at[pl.ds(0, 31)], late_got.at[pl.ds(0, 63)]
        send(out, out, LOUT, partner).wait_send()
        send(back, back, LBACK, partner).wait_send()

    @pl.when(odd == 1)
    def _():
        out = late_got.at[pl.ds(0, 32)]
        send(out, out, LOUT, partner).wait_send()

    for copy in started:
        copy.wait_send()


def exchange(vectors, active):
    rows, width = vectors.shape
    hbm = pl.BlockSpec(memory_space=pltpu.HBM)
    return pl.pallas_call(
        exchange_kernel,
        out_shape=(
            jax.ShapeDtypeStruct((2, 4, 4, 2, 8, 256), F32),
            jax.ShapeDtypeStruct((2, 16, 2, 8, 128), F32),
            jax.ShapeDtypeStruct((4, rows, width), BF16),
            jax.ShapeDtypeStruct((8, 512), F32),
        ),
        in_specs=[hbm, hbm],
        out_specs=(VMEM, VMEM, VMEM, VMEM),
        scratch_shapes=[
            pltpu.SMEM((8,), jnp.int32),
            pltpu.VMEM((2, rows // 2, width), BF16), pltpu.VMEM((4, rows // 4, width), BF16),
            pltpu.VMEM((256, 256), F32), pltpu.VMEM((128, 256), F32), pltpu.VMEM((3, 32, 256), F32),
            pltpu.VMEM((3, 8, 256), F32), pltpu.VMEM((4, 8, 256), F32),
            pltpu.VMEM((128, 256), F32), pltpu.VMEM((32, 256), F32), pltpu.VMEM((8, 256), F32),
            pltpu.VMEM((256, 256), F32), pltpu.VMEM((128, 256), F32), pltpu.VMEM((16, 2, 8, 128), F32),
            pltpu.VMEM((64, 8, 128), F32), pltpu.VMEM((256, 256), F32),
            pltpu.SemaphoreType.DMA((3,)), pltpu.SemaphoreType.DMA((SEMS,)), pltpu.SemaphoreType.DMA((SEMS,)),
        ],
        compiler_params=pltpu.CompilerParams(
            collective_id=0, has_side_effects=True, vmem_limit_bytes=24 * 2**20
        ),
        name="exchange",
    )(*[pltpu.with_memory_space_constraint(v, pltpu.HBM) for v in (vectors, active)])


def split(value):
    high = value.astype(BF16)
    return high, (value - high.astype(F32)).astype(BF16)


def product(left, right):
    (lh, ll), (rh, rl) = left, right
    return jnp.dot(
        jnp.concatenate([ll, lh, lh], axis=1), jnp.concatenate([rh, rl, rh], axis=0), preferred_element_type=F32
    )


def mirrored(left, right, below=None):
    h = left[0].shape[0] // 2
    upper = [v[:h] for v in left]
    if below is not None:
        upper = [jnp.concatenate(pair, axis=0) for pair in zip(upper, below)]
    top = product(upper, right)
    low = product([v[h:] for v in left], [v[:, h:] for v in right])
    top, rest = top[:h], top[h:]
    return jnp.concatenate([top, jnp.concatenate([top[:, h:].T, low], axis=1)], axis=0), rest


def narrow(left, right):
    (lh, ll), (rh, rl) = left, right
    rows = lh.shape[0]
    both = jnp.dot(jnp.concatenate([lh, ll], axis=0), rh, preferred_element_type=F32)
    return both[:rows] + (both[rows:] + jnp.dot(lh, rl, preferred_element_type=F32))


def finish_kernel(
    total_rows, early_ref, late_ref, all_ref, flag_ref, out_ref, matrix, result, out_sem,
):
    s = lax.axis_index("state")
    rows = all_ref.shape[1]
    cols = matrix.shape[0]
    cross = jnp.concatenate([late_ref[:, :, k].reshape(256, 128) for k in (0, 1)], axis=1)
    matrix[0:256, 0:256] = early_ref[:, :, :, 0].reshape(256, 256)
    matrix[256:512, 256:512] = early_ref[:, :, :, 1].reshape(256, 256)
    matrix[0:256, 256:512] = cross
    matrix[256:512, 0:256] = cross.T
    eye = lax.broadcasted_iota(jnp.int32, (cols, cols), 0) == lax.broadcasted_iota(jnp.int32, (cols, cols), 1)
    gram_matrix = matrix[...] + jnp.where(eye & (flag_ref[0:1, :] == 0.0), total_rows, 0.0)
    frob_norm = jnp.sqrt(jnp.sum(gram_matrix * gram_matrix, keepdims=True))
    current = gram_matrix / frob_norm

    rows_of = pl.ds(pl.multiple_of(s * 128, 128), 128)
    panel_eye = lax.broadcasted_iota(jnp.int32, (128, cols), 0) + s * 128 == lax.broadcasted_iota(jnp.int32, (128, cols), 1)

    def advance(parts, current, panel):
        square, moved = mirrored(parts, parts, None if panel is None else split(panel))
        first = 1.5 * current - 0.5 * square
        current = 1.5 * first - 0.5 * mirrored(split(first), parts)[0]
        if panel is not None:
            panel = 1.5 * panel - 0.5 * moved
        return split(current), current, panel

    matrix[...] = current
    first_panel = jnp.where(panel_eye, 1.5, 0.0) - 0.5 * matrix[rows_of, :]
    parts, current, _ = advance(split(current), current, None)
    parts, current, panel = advance(parts, current, first_panel)
    parts, current, panel = advance(parts, current, panel)
    panel = 1.5 * panel - 0.5 * narrow(split(panel), parts)
    last = narrow(split(panel), parts)
    last = 1.5 * last - 0.5 * narrow(split(last), parts)
    last = 1.5 * last - 0.5 * narrow(split(last), parts)
    panel = 1.5 * panel - 0.5 * last
    factor = (panel * jnp.sqrt(total_rows / frob_norm)).astype(BF16)
    keep = flag_ref[0:1, pl.ds(pl.multiple_of(s * 128, 128), 128)]
    chunk = 512
    for k in range(rows // chunk):
        block = pl.ds(k * chunk, chunk)
        left = jnp.concatenate([all_ref[k4, block] for k4 in range(4)], axis=1)
        value = lax.dot_general(left, factor, (((1,), (1,)), ((), ())), preferred_element_type=F32)
        result[block] = jnp.where(keep == 1.0, value, all_ref[s, block].astype(F32)).astype(BF16)
        pltpu.make_async_copy(result.at[block], out_ref.at[block], out_sem.at[k]).start()
    for k in range(rows // chunk):
        block = pl.ds(k * chunk, chunk)
        pltpu.make_async_copy(result.at[block], out_ref.at[block], out_sem.at[k]).wait()


def finish(total_rows, early, late, everything, flag):
    rows, width = everything.shape[1:]
    return pl.pallas_call(
        functools.partial(finish_kernel, total_rows),
        out_shape=jax.ShapeDtypeStruct((rows, width), BF16),
        in_specs=[VMEM] * 4,
        out_specs=ANY,
        scratch_shapes=[
            pltpu.VMEM((512, 512), F32), pltpu.VMEM((rows, width), BF16),
            pltpu.SemaphoreType.DMA((8,)),
        ],
        compiler_params=pltpu.CompilerParams(vmem_limit_bytes=40 * 2**20),
        name="finish",
    )(early, late, everything, flag)


def shards(vectors, active):
    total_rows = float(vectors.shape[0] * lax.axis_size("row"))
    return finish(total_rows, *exchange(vectors, active))


def solution(mesh):
    in_specs = (P("row", "state"), P())
    out_specs = P("row", "state")
    return jax.shard_map(shards, mesh=mesh, in_specs=in_specs, out_specs=out_specs, check_vma=False)
```

```python
import functools

import jax
import jax.numpy as jnp
from jax import lax
from jax.experimental import pallas as pl
from jax.experimental.pallas import tpu as pltpu
from jax.sharding import PartitionSpec as P

VECS = 64
MESH = pl.DeviceIdType.MESH
F32 = jnp.float32
BF16 = jnp.bfloat16
ANY = pl.BlockSpec(memory_space=pl.ANY)
VMEM = pl.BlockSpec(memory_space=pltpu.VMEM)

HALF, OWN, CORE, PLANE, PBACK, ZDIM, CBACK, LCORE, LOUT, LBACK, LCBACK = 0, 1, 2, 3, 4, 5, 8, 9, 10, 11, 12
LINK, RELAY, QUARTER, SEMS = 13, 29, 45, 61
CHUNKS = 8
FIRST = 8
PLAN = ((0,), (1, 2, 3, 4), (5, 6, 7))
OFFSETS = [(a, b, d) for a in range(4) for b in range(4) for d in range(4)]


def hops(offset):
    return sum(min(v, 4 - v) for v in offset)


def gram(left, right):
    return lax.dot_general(left, right, (((0,), (0,)), ((), ())), preferred_element_type=F32)


def exchange_kernel(
    vec_ref, active_hbm, early_ref, late_ref, all_ref, flag_ref,
    active, quart, early_got, early_z, early_sum, early_own,
    late_part, late_core, late_sum, late_got, mask, local_sem, send_sem, recv_sem, ready,
):
    s, r = lax.axis_index("state"), lax.axis_index("row")
    zh, c = s // 2, s % 2
    zl, x, y = r // 16, (r // 4) % 4, r % 4
    z = zh * 2 + zl
    other_r = r + 16 * (1 - 2 * zl)
    near = s + 1 - 2 * c
    partner = (near, r)
    far = 2 - 2 * zh
    rows = vec_ref.shape[0]
    quart_rows = rows // 4

    xs = [lax.rem(x + a, 4) * 4 for a in range(4)]
    ys = [lax.rem(y + b, 4) for b in range(4)]
    zs = [lax.rem(z + d, 4) for d in range(4)]
    states = [lax.div(to, 2) * 2 + c for to in zs]
    lows = [lax.rem(to, 2) * 16 for to in zs]
    spots = [[to_x + to_y for to_y in ys] for to_x in xs]

    def device(offset):
        a, b, d = offset
        return (states[d], lows[d] + spots[a][b])

    def x_peer(d):
        return device((d, 0, 0))

    def y_peer(d):
        return device((0, d, 0))

    def z_peer(d):
        return device((0, 0, d))

    def send(src, dst, sem, to, recv=None):
        return pltpu.make_async_remote_copy(
            src_ref=src, dst_ref=dst, send_sem=send_sem.at[sem],
            recv_sem=recv_sem.at[sem if recv is None else recv],
            device_id=to, device_id_type=MESH,
        )

    started = []

    def start(copies, wait=True):
        for copy in copies:
            copy.start()
        if wait:
            started.extend(copies)
        return copies

    def arrive(copies):
        for copy in copies:
            copy.wait_recv()

    flag_copy = pltpu.make_async_copy(active_hbm, active, local_sem.at[1])
    flag_copy.start()
    own = pltpu.make_async_copy(vec_ref, all_ref.at[s], local_sem.at[2])
    own.start()

    barrier = pltpu.get_barrier_semaphore()
    peers = [partner] + [(t, other_r) for t in range(4)] + [z_peer(2)]
    peers += [x_peer(d) for d in (1, 2, 3)] + [y_peer(d) for d in (1, 2, 3)]
    for peer in peers:
        pl.semaphore_signal(barrier, inc=1, device_id=peer, device_id_type=MESH)
    pl.semaphore_wait(barrier, len(peers))

    start([send(vec_ref, all_ref.at[s], OWN, partner)])
    edges = [0, FIRST * quart_rows // 16, quart_rows]
    pieces = [pl.ds(edges[k], edges[k + 1] - edges[k]) for k in (0, 1)]

    def quarter(piece, t, frm):
        return send(
            vec_ref.at[pl.ds(t * quart_rows + edges[piece], edges[piece + 1] - edges[piece])],
            quart.at[frm, pieces[piece]], QUARTER + piece * 4 + t, (t, other_r), recv=QUARTER + piece * 4 + frm,
        )

    for piece in (0, 1):
        start([quarter(piece, t, s) for t in range(4)])
    for d in (1, 2, 3):
        pl.semaphore_signal(ready, inc=1, device_id=x_peer(d), device_id_type=MESH)

    flag_copy.wait()

    def flags(shape, axis, first):
        state = lax.broadcasted_iota(jnp.int32, shape, axis) // VECS + first
        flag = jnp.zeros(shape, F32)
        for k in range(8):
            flag = jnp.where(state == k, active[k].astype(F32), flag)
        return flag

    flag_ref[...] = flags(flag_ref.shape, 1, 0)
    block = (256, 256)
    mask[...] = flags(block, 0, 0) * flags(block, 1, 4)
    early_mask = flags((128, 256), 0, s * 2) * flags((128, 256), 1, zh * 4)

    own.wait()
    send(vec_ref, all_ref.at[near], OWN, partner).wait_recv()
    both = jnp.concatenate([all_ref[s - c], all_ref[s - c + 1]], axis=1)
    total = jnp.where(early_mask == 1.0, gram(all_ref[s], both), 0.0)
    early_sum[...] = total.reshape(16, 8, 256)
    pl.semaphore_wait(ready, 3)
    spot = x * 4 + y
    plane = sorted([(a, b, 0) for a in range(4) for b in range(4) if a or b], key=hops, reverse=True)
    start([
        send(early_sum.at[((x + a) % 4) * 4 + (y + b) % 4], early_got.at[spot], PLANE, device((a, b, 0)))
        for a, b, _ in plane
    ], False)
    early_got[spot] = early_sum[spot]
    fifteen = early_got.at[pl.ds(0, 15)]
    send(fifteen, fifteen, PLANE, partner).wait_recv()
    early_own[...] = jnp.sum(early_got[...], axis=0)
    early_z[z] = early_own[...]
    early_step = start([send(early_own, early_z.at[z], ZDIM + d - 1, z_peer(d)) for d in (1, 2, 3)])

    chunk_rows = 2 * quart_rows // CHUNKS

    def chunk_at(chunk, core, frm):
        part, piece = chunk // (CHUNKS // 2), chunk % (CHUNKS // 2)
        return all_ref.at[far + part, pl.ds((frm * 2 + core) * quart_rows + piece * chunk_rows, chunk_rows)]

    def link(chunk):
        part, piece = chunk // (CHUNKS // 2), chunk % (CHUNKS // 2)
        return [
            send(
                quart.at[2 - 2 * to + part, pl.ds(piece * chunk_rows, chunk_rows)],
                all_ref.at[2 - 2 * to + part, pl.ds(s * quart_rows + piece * chunk_rows, chunk_rows)],
                LINK + chunk * 2 + to, (to * 2 + c, other_r), recv=LINK + chunk * 2 + zh,
            )
            for to in (0, 1)
        ]

    def relay_copies(chunk, core):
        blocks = [chunk_at(chunk, core, frm) for frm in (0, 1)]
        return [send(block, block, RELAY + chunk * 2 + frm, partner) for frm, block in enumerate(blocks)]

    def relay(chunk):
        for frm in (0, 1):
            block = chunk_at(chunk, c, frm)
            send(block, block, LINK + chunk * 2 + frm, partner).wait_recv()
        start(relay_copies(chunk, c))

    for piece in (0, 1):
        arrive([quarter(piece, 0, t) for t in range(4)])
    for chunk in PLAN[0]:
        start(link(chunk))
    left = jnp.concatenate([quart[0], quart[1]], axis=1)
    right = jnp.concatenate([quart[2], quart[3]], axis=1)
    late_part[...] = jnp.where(mask[...] == 1.0, gram(left, right), 0.0)
    step = start([send(late_part.at[pl.ds((1 - c) * 128, 128)], late_core, LCORE, partner)])
    arrive(step)
    total = late_part[pl.ds(pl.multiple_of(c * 128, 128), 128), :] + late_core[...]
    for k in (0, 1):
        late_sum[:, k] = total[:, k * 128:(k + 1) * 128].reshape(16, 8, 128)
    odd = (x + y + z + c) % 2
    place = x * 16 + y * 4 + z
    outward = sorted([(a, b, d) for a in range(4) for b in range(4) for d in (0, 2)], key=hops, reverse=True)

    owner_z = [[lax.rem(z + d + even, 4) for even in (odd, 1 - odd)] for d in (0, 2)]
    owner_state = [[lax.div(to, 2) * 2 + c for to in pair] for pair in owner_z]
    owner_low = [[lax.rem(to, 2) * 16 for to in pair] for pair in owner_z]
    owner_half = [[lax.div(to, 2) for to in pair] for pair in owner_z]

    def scatter(offset):
        a, b, d = offset
        k, even, spot_to = d // 2, (a + b) % 2, spots[a][b]
        send(
            late_sum.at[spot_to, owner_half[k][even]], late_got.at[place], LOUT,
            (owner_state[k][even], owner_low[k][even] + spot_to),
        ).start()

    for offset in outward:
        if offset == (0, 0, 0):
            pl.when(odd == 1)(functools.partial(scatter, offset))
        else:
            scatter(offset)
    for chunk in PLAN[1]:
        start(link(chunk))
    arrive(early_step)
    early_ref[c, spot, 0] = early_z[0] + early_z[1]
    early_ref[c, spot, 1] = early_z[2] + early_z[3]
    start([send(early_ref.at[c, spot], early_ref.at[c, spot], PBACK, device(offset)) for offset in plane], False)
    for chunk in PLAN[0]:
        relay(chunk)

    here = (c, x * 4 + y, z // 2)

    @pl.when(odd == 0)
    def _():
        late_got[place] = late_sum[x * 4 + y, z // 2]
        whole = late_got.at[pl.ds(0, 63)]
        send(whole, whole, LOUT, partner).wait_recv()
        late_ref[here] = jnp.sum(late_got[...], axis=0)
        for offset in sorted(OFFSETS[1:], key=hops, reverse=True):
            send(late_ref.at[here], late_ref.at[here], LBACK, device(offset)).start()

    for chunk in PLAN[2]:
        start(link(chunk))
    for chunk in PLAN[1]:
        relay(chunk)
    fifteen = early_ref.at[c, pl.ds(0, 15)]
    send(fifteen, fifteen, PBACK, partner).wait_recv()
    early_step = start([send(early_ref.at[c], early_ref.at[c], CBACK, partner)])

    @pl.when(odd == 0)
    def _():
        gathered = late_got.at[pl.ds(0, 31)]
        send(gathered, gathered, LBACK, partner).wait_recv()

    @pl.when(odd == 1)
    def _():
        gathered = late_got.at[pl.ds(0, 32)]
        send(gathered, gathered, LBACK, partner).wait_recv()

    step = start([send(late_ref.at[c], late_ref.at[c], LCBACK, partner)])
    for chunk in PLAN[2]:
        relay(chunk)
    arrive(early_step)
    arrive(step)
    for chunk in range(CHUNKS):
        arrive(relay_copies(chunk, 1 - c))

    @pl.when(odd == 0)
    def _():
        out, back = late_got.at[pl.ds(0, 31)], late_got.at[pl.ds(0, 63)]
        send(out, out, LOUT, partner).wait_send()
        send(back, back, LBACK, partner).wait_send()

    @pl.when(odd == 1)
    def _():
        out = late_got.at[pl.ds(0, 32)]
        send(out, out, LOUT, partner).wait_send()

    send(fifteen, fifteen, PBACK, partner).wait_send()
    fifteen = early_got.at[pl.ds(0, 15)]
    send(fifteen, fifteen, PLANE, partner).wait_send()
    for copy in started:
        copy.wait_send()


def exchange(vectors, active):
    rows, width = vectors.shape
    hbm = pl.BlockSpec(memory_space=pltpu.HBM)
    return pl.pallas_call(
        exchange_kernel,
        out_shape=(
            jax.ShapeDtypeStruct((2, 16, 2, 8, 256), F32),
            jax.ShapeDtypeStruct((2, 16, 2, 8, 128), F32),
            jax.ShapeDtypeStruct((4, rows, width), BF16),
            jax.ShapeDtypeStruct((8, 512), F32),
        ),
        in_specs=[hbm, hbm],
        out_specs=(VMEM, VMEM, VMEM, VMEM),
        scratch_shapes=[
            pltpu.SMEM((8,), jnp.int32),
            pltpu.VMEM((4, rows // 4, width), BF16), pltpu.VMEM((16, 8, 256), F32),
            pltpu.VMEM((4, 8, 256), F32), pltpu.VMEM((16, 8, 256), F32), pltpu.VMEM((8, 256), F32),
            pltpu.VMEM((256, 256), F32), pltpu.VMEM((128, 256), F32), pltpu.VMEM((16, 2, 8, 128), F32),
            pltpu.VMEM((64, 8, 128), F32), pltpu.VMEM((256, 256), F32),
            pltpu.SemaphoreType.DMA((3,)), pltpu.SemaphoreType.DMA((SEMS,)), pltpu.SemaphoreType.DMA((SEMS,)),
            pltpu.SemaphoreType.REGULAR,
        ],
        compiler_params=pltpu.CompilerParams(
            collective_id=0, has_side_effects=True, vmem_limit_bytes=24 * 2**20
        ),
        name="exchange",
    )(*[pltpu.with_memory_space_constraint(v, pltpu.HBM) for v in (vectors, active)])


def split(value):
    high = value.astype(BF16)
    return high, (value - high.astype(F32)).astype(BF16)


def product(left, right):
    (lh, ll), (rh, rl) = left, right
    return jnp.dot(
        jnp.concatenate([ll, lh, lh], axis=1), jnp.concatenate([rh, rl, rh], axis=0), preferred_element_type=F32
    )


def mirrored(left, right, below=None):
    h = left[0].shape[0] // 2
    upper = [v[:h] for v in left]
    if below is not None:
        upper = [jnp.concatenate(pair, axis=0) for pair in zip(upper, below)]
    top = product(upper, right)
    low = product([v[h:] for v in left], [v[:, h:] for v in right])
    top, rest = top[:h], top[h:]
    return jnp.concatenate([top, jnp.concatenate([top[:, h:].T, low], axis=1)], axis=0), rest


def narrow(left, right):
    (lh, ll), (rh, rl) = left, right
    rows = lh.shape[0]
    both = jnp.dot(jnp.concatenate([lh, ll], axis=0), rh, preferred_element_type=F32)
    return both[:rows] + (both[rows:] + jnp.dot(lh, rl, preferred_element_type=F32))


def finish_kernel(
    total_rows, early_ref, late_ref, all_ref, flag_ref, out_ref, matrix, result, out_sem,
):
    s = lax.axis_index("state")
    rows = all_ref.shape[1]
    cols = matrix.shape[0]
    cross = jnp.concatenate([late_ref[:, :, k].reshape(256, 128) for k in (0, 1)], axis=1)
    matrix[0:256, 0:256] = early_ref[:, :, 0].reshape(256, 256)
    matrix[256:512, 256:512] = early_ref[:, :, 1].reshape(256, 256)
    matrix[0:256, 256:512] = cross
    matrix[256:512, 0:256] = cross.T
    eye = lax.broadcasted_iota(jnp.int32, (cols, cols), 0) == lax.broadcasted_iota(jnp.int32, (cols, cols), 1)
    gram_matrix = matrix[...] + jnp.where(eye & (flag_ref[0:1, :] == 0.0), total_rows, 0.0)
    frob_norm = jnp.sqrt(jnp.sum(gram_matrix * gram_matrix, keepdims=True))
    current = gram_matrix / frob_norm

    rows_of = pl.ds(pl.multiple_of(s * 128, 128), 128)
    panel_eye = lax.broadcasted_iota(jnp.int32, (128, cols), 0) + s * 128 == lax.broadcasted_iota(jnp.int32, (128, cols), 1)

    def advance(parts, current, panel):
        square, moved = mirrored(parts, parts, None if panel is None else split(panel))
        first = 1.5 * current - 0.5 * square
        current = 1.5 * first - 0.5 * mirrored(split(first), parts)[0]
        if panel is not None:
            panel = 1.5 * panel - 0.5 * moved
        return split(current), current, panel

    matrix[...] = current
    first_panel = jnp.where(panel_eye, 1.5, 0.0) - 0.5 * matrix[rows_of, :]
    parts, current, _ = advance(split(current), current, None)
    parts, current, panel = advance(parts, current, first_panel)
    parts, current, panel = advance(parts, current, panel)
    panel = 1.5 * panel - 0.5 * narrow(split(panel), parts)
    last = narrow(split(panel), parts)
    last = 1.5 * last - 0.5 * narrow(split(last), parts)
    last = 1.5 * last - 0.5 * narrow(split(last), parts)
    panel = 1.5 * panel - 0.5 * last
    factor = (panel * jnp.sqrt(total_rows / frob_norm)).astype(BF16)
    keep = flag_ref[0:1, pl.ds(pl.multiple_of(s * 128, 128), 128)]
    chunk = 512
    for k in range(rows // chunk):
        block = pl.ds(k * chunk, chunk)
        left = jnp.concatenate([all_ref[k4, block] for k4 in range(4)], axis=1)
        value = lax.dot_general(left, factor, (((1,), (1,)), ((), ())), preferred_element_type=F32)
        result[block] = jnp.where(keep == 1.0, value, all_ref[s, block].astype(F32)).astype(BF16)
        pltpu.make_async_copy(result.at[block], out_ref.at[block], out_sem.at[k]).start()
    for k in range(rows // chunk):
        block = pl.ds(k * chunk, chunk)
        pltpu.make_async_copy(result.at[block], out_ref.at[block], out_sem.at[k]).wait()


def finish(total_rows, early, late, everything, flag):
    rows, width = everything.shape[1:]
    return pl.pallas_call(
        functools.partial(finish_kernel, total_rows),
        out_shape=jax.ShapeDtypeStruct((rows, width), BF16),
        in_specs=[VMEM] * 4,
        out_specs=ANY,
        scratch_shapes=[
            pltpu.VMEM((512, 512), F32), pltpu.VMEM((rows, width), BF16),
            pltpu.SemaphoreType.DMA((8,)),
        ],
        compiler_params=pltpu.CompilerParams(vmem_limit_bytes=40 * 2**20),
        name="finish",
    )(early, late, everything, flag)


def shards(vectors, active):
    total_rows = float(vectors.shape[0] * lax.axis_size("row"))
    return finish(total_rows, *exchange(vectors, active))


def solution(mesh):
    in_specs = (P("row", "state"), P())
    out_specs = P("row", "state")
    return jax.shard_map(shards, mesh=mesh, in_specs=in_specs, out_specs=out_specs, check_vma=False)
```

```python
import functools

import jax
import jax.numpy as jnp
from jax import lax
from jax.experimental import pallas as pl
from jax.experimental.pallas import tpu as pltpu
from jax.sharding import PartitionSpec as P

VECS = 64
MESH = pl.DeviceIdType.MESH
F32 = jnp.float32
BF16 = jnp.bfloat16
ANY = pl.BlockSpec(memory_space=pl.ANY)
VMEM = pl.BlockSpec(memory_space=pltpu.VMEM)

HALF, OWN, CORE, PLANE, PBACK, ZDIM, CBACK, LCORE, LOUT, LBACK, LCBACK = 0, 1, 2, 3, 4, 5, 8, 9, 10, 11, 12
LINK, RELAY, QUARTER, SEMS = 13, 29, 45, 61
CHUNKS = 8
FIRST = 8
PLAN = ((0, 1, 2), (3, 4, 5), (6, 7))
OFFSETS = [(a, b, d) for a in range(4) for b in range(4) for d in range(4)]


def hops(offset):
    return sum(min(v, 4 - v) for v in offset)


def gram(left, right):
    return lax.dot_general(left, right, (((0,), (0,)), ((), ())), preferred_element_type=F32)


def split(value):
    high = value.astype(BF16)
    return high, (value - high.astype(F32)).astype(BF16)


def product(left, right):
    (lh, ll), (rh, rl) = left, right
    return jnp.dot(
        jnp.concatenate([ll, lh, lh], axis=1), jnp.concatenate([rh, rl, rh], axis=0), preferred_element_type=F32
    )


def mirrored(left, right, below=None):
    h = left[0].shape[0] // 2
    upper = [v[:h] for v in left]
    if below is not None:
        upper = [jnp.concatenate(pair, axis=0) for pair in zip(upper, below)]
    top = product(upper, right)
    low = product([v[h:] for v in left], [v[:, h:] for v in right])
    top, rest = top[:h], top[h:]
    return jnp.concatenate([top, jnp.concatenate([top[:, h:].T, low], axis=1)], axis=0), rest


def exchange_kernel(
    total_rows, vec_ref, active_hbm, blocks_ref, parts_ref, squares_ref, scale_ref, late_ref, all_ref, flag_ref,
    early_ref, active, quart, early_got, early_z, early_sum, early_own,
    late_part, late_core, late_sum, late_got, mask, local_sem, send_sem, recv_sem, ready,
):
    s, r = lax.axis_index("state"), lax.axis_index("row")
    zh, c = s // 2, s % 2
    zl, x, y = r // 16, (r // 4) % 4, r % 4
    z = zh * 2 + zl
    other_r = r + 16 * (1 - 2 * zl)
    near = s + 1 - 2 * c
    partner = (near, r)
    far = 2 - 2 * zh
    rows = vec_ref.shape[0]
    quart_rows = rows // 4

    xs = [lax.rem(x + a, 4) * 4 for a in range(4)]
    ys = [lax.rem(y + b, 4) for b in range(4)]
    zs = [lax.rem(z + d, 4) for d in range(4)]
    states = [lax.div(to, 2) * 2 + c for to in zs]
    lows = [lax.rem(to, 2) * 16 for to in zs]
    spots = [[to_x + to_y for to_y in ys] for to_x in xs]

    def device(offset):
        a, b, d = offset
        return (states[d], lows[d] + spots[a][b])

    def x_peer(d):
        return device((d, 0, 0))

    def y_peer(d):
        return device((0, d, 0))

    def z_peer(d):
        return device((0, 0, d))

    def send(src, dst, sem, to, recv=None):
        return pltpu.make_async_remote_copy(
            src_ref=src, dst_ref=dst, send_sem=send_sem.at[sem],
            recv_sem=recv_sem.at[sem if recv is None else recv],
            device_id=to, device_id_type=MESH,
        )

    started = []

    def start(copies, wait=True):
        for copy in copies:
            copy.start()
        if wait:
            started.extend(copies)
        return copies

    def arrive(copies):
        for copy in copies:
            copy.wait_recv()

    flag_copy = pltpu.make_async_copy(active_hbm, active, local_sem.at[1])
    flag_copy.start()
    own = pltpu.make_async_copy(vec_ref, all_ref.at[s], local_sem.at[2])
    own.start()

    barrier = pltpu.get_barrier_semaphore()
    peers = [partner] + [(t, other_r) for t in range(4)] + [z_peer(2)]
    peers += [x_peer(d) for d in (1, 2, 3)] + [y_peer(d) for d in (1, 2, 3)]
    for peer in peers:
        pl.semaphore_signal(barrier, inc=1, device_id=peer, device_id_type=MESH)
    pl.semaphore_wait(barrier, len(peers))

    start([send(vec_ref, all_ref.at[s], OWN, partner)])
    edges = [0, FIRST * quart_rows // 16, quart_rows]
    pieces = [pl.ds(edges[k], edges[k + 1] - edges[k]) for k in (0, 1)]

    def quarter(piece, t, frm):
        return send(
            vec_ref.at[pl.ds(t * quart_rows + edges[piece], edges[piece + 1] - edges[piece])],
            quart.at[frm, pieces[piece]], QUARTER + piece * 4 + t, (t, other_r), recv=QUARTER + piece * 4 + frm,
        )

    for piece in (0, 1):
        start([quarter(piece, t, s) for t in range(4)])
    for d in (1, 2, 3):
        pl.semaphore_signal(ready, inc=1, device_id=x_peer(d), device_id_type=MESH)

    flag_copy.wait()

    def flags(shape, axis, first):
        state = lax.broadcasted_iota(jnp.int32, shape, axis) // VECS + first
        flag = jnp.zeros(shape, F32)
        for k in range(8):
            flag = jnp.where(state == k, active[k].astype(F32), flag)
        return flag

    flag_ref[...] = flags(flag_ref.shape, 1, 0)
    block = (256, 256)
    mask[...] = flags(block, 0, 0) * flags(block, 1, 4)
    early_mask = flags((128, 256), 0, s * 2) * flags((128, 256), 1, zh * 4)

    own.wait()
    send(vec_ref, all_ref.at[near], OWN, partner).wait_recv()
    both = jnp.concatenate([all_ref[s - c], all_ref[s - c + 1]], axis=1)
    total = jnp.where(early_mask == 1.0, gram(all_ref[s], both), 0.0)
    early_sum[...] = total.reshape(16, 8, 256)
    pl.semaphore_wait(ready, 3)
    spot = x * 4 + y
    plane = sorted([(a, b, 0) for a in range(4) for b in range(4) if a or b], key=hops, reverse=True)
    start([
        send(early_sum.at[((x + a) % 4) * 4 + (y + b) % 4], early_got.at[spot], PLANE, device((a, b, 0)))
        for a, b, _ in plane
    ], False)
    early_got[spot] = early_sum[spot]
    fifteen = early_got.at[pl.ds(0, 15)]
    send(fifteen, fifteen, PLANE, partner).wait_recv()
    early_own[...] = jnp.sum(early_got[...], axis=0)
    early_z[z] = early_own[...]
    early_step = start([send(early_own, early_z.at[z], ZDIM + d - 1, z_peer(d)) for d in (1, 2, 3)])

    chunk_rows = 2 * quart_rows // CHUNKS

    def chunk_at(chunk, core, frm):
        part, piece = chunk // (CHUNKS // 2), chunk % (CHUNKS // 2)
        return all_ref.at[far + part, pl.ds((frm * 2 + core) * quart_rows + piece * chunk_rows, chunk_rows)]

    def link(chunk):
        part, piece = chunk // (CHUNKS // 2), chunk % (CHUNKS // 2)
        return [
            send(
                quart.at[2 - 2 * to + part, pl.ds(piece * chunk_rows, chunk_rows)],
                all_ref.at[2 - 2 * to + part, pl.ds(s * quart_rows + piece * chunk_rows, chunk_rows)],
                LINK + chunk * 2 + to, (to * 2 + c, other_r), recv=LINK + chunk * 2 + zh,
            )
            for to in (0, 1)
        ]

    def relay_copies(chunk, core):
        blocks = [chunk_at(chunk, core, frm) for frm in (0, 1)]
        return [send(block, block, RELAY + chunk * 2 + frm, partner) for frm, block in enumerate(blocks)]

    def relay(chunk):
        for frm in (0, 1):
            block = chunk_at(chunk, c, frm)
            send(block, block, LINK + chunk * 2 + frm, partner).wait_recv()
        start(relay_copies(chunk, c))

    for piece in (0, 1):
        arrive([quarter(piece, 0, t) for t in range(4)])
    for chunk in PLAN[0]:
        start(link(chunk))
    left = jnp.concatenate([quart[0], quart[1]], axis=1)
    right = jnp.concatenate([quart[2], quart[3]], axis=1)
    late_part[...] = jnp.where(mask[...] == 1.0, gram(left, right), 0.0)
    step = start([send(late_part.at[pl.ds((1 - c) * 128, 128)], late_core, LCORE, partner)])
    arrive(step)
    total = late_part[pl.ds(pl.multiple_of(c * 128, 128), 128), :] + late_core[...]
    for k in (0, 1):
        late_sum[:, k] = total[:, k * 128:(k + 1) * 128].reshape(16, 8, 128)
    odd = (x + y + z + c) % 2
    place = x * 16 + y * 4 + z
    outward = sorted([(a, b, d) for a in range(4) for b in range(4) for d in (0, 2)], key=hops, reverse=True)

    owner_z = [[lax.rem(z + d + even, 4) for even in (odd, 1 - odd)] for d in (0, 2)]
    owner_state = [[lax.div(to, 2) * 2 + c for to in pair] for pair in owner_z]
    owner_low = [[lax.rem(to, 2) * 16 for to in pair] for pair in owner_z]
    owner_half = [[lax.div(to, 2) for to in pair] for pair in owner_z]

    def scatter(offset):
        a, b, d = offset
        k, even, spot_to = d // 2, (a + b) % 2, spots[a][b]
        send(
            late_sum.at[spot_to, owner_half[k][even]], late_got.at[place], LOUT,
            (owner_state[k][even], owner_low[k][even] + spot_to),
        ).start()

    for offset in outward:
        if offset == (0, 0, 0):
            pl.when(odd == 1)(functools.partial(scatter, offset))
        else:
            scatter(offset)
    for chunk in PLAN[1]:
        start(link(chunk))
    arrive(early_step)
    early_ref[c, spot, 0] = early_z[0] + early_z[1]
    early_ref[c, spot, 1] = early_z[2] + early_z[3]
    start([send(early_ref.at[c, spot], early_ref.at[c, spot], PBACK, device(offset)) for offset in plane], False)
    for chunk in PLAN[0]:
        relay(chunk)

    here = (c, x * 4 + y, z // 2)

    @pl.when(odd == 0)
    def _():
        late_got[place] = late_sum[x * 4 + y, z // 2]
        whole = late_got.at[pl.ds(0, 63)]
        send(whole, whole, LOUT, partner).wait_recv()
        late_ref[here] = jnp.sum(late_got[...], axis=0)
        for offset in sorted(OFFSETS[1:], key=hops, reverse=True):
            send(late_ref.at[here], late_ref.at[here], LBACK, device(offset)).start()

    for chunk in PLAN[2]:
        start(link(chunk))
    for chunk in PLAN[1]:
        relay(chunk)
    fifteen = early_ref.at[c, pl.ds(0, 15)]
    send(fifteen, fifteen, PBACK, partner).wait_recv()
    early_step = start([send(early_ref.at[c], early_ref.at[c], CBACK, partner)])

    arrive(early_step)
    diagonal = lax.broadcasted_iota(jnp.int32, (256, 256), 0) == lax.broadcasted_iota(jnp.int32, (256, 256), 1)
    values = []
    for k in (0, 1):
        idle = diagonal & (flag_ref[0:1, k * 256:k * 256 + 256] == 0.0)
        values.append(early_ref[:, :, k].reshape(256, 256) + jnp.where(idle, total_rows, 0.0))
    largest = jnp.maximum(*[jnp.max(value, keepdims=True) for value in values])
    scale_ref[...] = jnp.broadcast_to(1.0 / largest, scale_ref.shape)
    for k in (0, 1):
        value = values[k] * scale_ref[0:1, 0:1]
        high, low = split(value)
        blocks_ref[k] = value
        parts_ref[0, k] = high
        parts_ref[1, k] = low
        squares_ref[k] = product((high, low), (high, low))

    @pl.when(odd == 0)
    def _():
        gathered = late_got.at[pl.ds(0, 31)]
        send(gathered, gathered, LBACK, partner).wait_recv()

    @pl.when(odd == 1)
    def _():
        gathered = late_got.at[pl.ds(0, 32)]
        send(gathered, gathered, LBACK, partner).wait_recv()

    step = start([send(late_ref.at[c], late_ref.at[c], LCBACK, partner)])
    for chunk in PLAN[2]:
        relay(chunk)
    arrive(step)
    for chunk in range(CHUNKS):
        arrive(relay_copies(chunk, 1 - c))

    @pl.when(odd == 0)
    def _():
        out, back = late_got.at[pl.ds(0, 31)], late_got.at[pl.ds(0, 63)]
        send(out, out, LOUT, partner).wait_send()
        send(back, back, LBACK, partner).wait_send()

    @pl.when(odd == 1)
    def _():
        out = late_got.at[pl.ds(0, 32)]
        send(out, out, LOUT, partner).wait_send()

    send(fifteen, fifteen, PBACK, partner).wait_send()
    fifteen = early_got.at[pl.ds(0, 15)]
    send(fifteen, fifteen, PLANE, partner).wait_send()
    for copy in started:
        copy.wait_send()


def exchange(total_rows, vectors, active):
    rows, width = vectors.shape
    hbm = pl.BlockSpec(memory_space=pltpu.HBM)
    return pl.pallas_call(
        functools.partial(exchange_kernel, total_rows),
        out_shape=(
            jax.ShapeDtypeStruct((2, 256, 256), F32),
            jax.ShapeDtypeStruct((2, 2, 256, 256), BF16),
            jax.ShapeDtypeStruct((2, 256, 256), F32),
            jax.ShapeDtypeStruct((8, 128), F32),
            jax.ShapeDtypeStruct((2, 16, 2, 8, 128), F32),
            jax.ShapeDtypeStruct((4, rows, width), BF16),
            jax.ShapeDtypeStruct((8, 512), F32),
        ),
        in_specs=[hbm, hbm],
        out_specs=(VMEM,) * 7,
        scratch_shapes=[
            pltpu.VMEM((2, 16, 2, 8, 256), F32),
            pltpu.SMEM((8,), jnp.int32),
            pltpu.VMEM((4, rows // 4, width), BF16), pltpu.VMEM((16, 8, 256), F32),
            pltpu.VMEM((4, 8, 256), F32), pltpu.VMEM((16, 8, 256), F32), pltpu.VMEM((8, 256), F32),
            pltpu.VMEM((256, 256), F32), pltpu.VMEM((128, 256), F32), pltpu.VMEM((16, 2, 8, 128), F32),
            pltpu.VMEM((64, 8, 128), F32), pltpu.VMEM((256, 256), F32),
            pltpu.SemaphoreType.DMA((3,)), pltpu.SemaphoreType.DMA((SEMS,)), pltpu.SemaphoreType.DMA((SEMS,)),
            pltpu.SemaphoreType.REGULAR,
        ],
        compiler_params=pltpu.CompilerParams(
            collective_id=0, has_side_effects=True, vmem_limit_bytes=24 * 2**20
        ),
        name="exchange",
    )(*[pltpu.with_memory_space_constraint(v, pltpu.HBM) for v in (vectors, active)])


def narrow(left, right):
    (lh, ll), (rh, rl) = left, right
    rows = lh.shape[0]
    both = jnp.dot(jnp.concatenate([lh, ll], axis=0), rh, preferred_element_type=F32)
    return both[:rows] + (both[rows:] + jnp.dot(lh, rl, preferred_element_type=F32))


def finish_kernel(
    total_rows, blocks_ref, parts_ref, squares_ref, scale_ref, late_ref, all_ref, flag_ref, out_ref, matrix, result, out_sem,
):
    s = lax.axis_index("state")
    rows = all_ref.shape[1]
    cols = matrix.shape[0]
    scale = scale_ref[0:1, 0:1]
    cross = jnp.concatenate([late_ref[:, :, k].reshape(256, 128) for k in (0, 1)], axis=1) * scale
    turned = cross.T
    one, two = blocks_ref[0], blocks_ref[1]
    frob_norm = jnp.sqrt(
        jnp.sum(one * one, keepdims=True) + jnp.sum(two * two, keepdims=True) + 2.0 * jnp.sum(cross * cross, keepdims=True)
    )
    inverse_norm = 1.0 / frob_norm
    cross_parts, turned_parts = split(cross), split(turned)
    corner = product(
        [jnp.concatenate([parts_ref[k, 0], cross_parts[k]], axis=1) for k in (0, 1)],
        [jnp.concatenate([cross_parts[k], parts_ref[k, 1]], axis=0) for k in (0, 1)],
    )
    upper = squares_ref[0] + product(cross_parts, turned_parts)
    lower = squares_ref[1] + product(turned_parts, cross_parts)

    def whole(first, second, third, fourth):
        return jnp.concatenate(
            [jnp.concatenate([first, second], axis=1), jnp.concatenate([third, fourth], axis=1)], axis=0
        )

    current = whole(one, cross, turned, two) * inverse_norm
    square = whole(upper, corner, corner.T, lower) * inverse_norm * inverse_norm
    rows_of = pl.ds(pl.multiple_of(s * 128, 128), 128)
    panel_eye = lax.broadcasted_iota(jnp.int32, (128, cols), 0) + s * 128 == lax.broadcasted_iota(jnp.int32, (128, cols), 1)

    def advance(parts, current, panel, square=None):
        if square is None:
            square, moved = mirrored(parts, parts, split(panel))
        first = 1.5 * current - 0.5 * square
        current = 1.5 * first - 0.5 * mirrored(split(first), parts)[0]
        if panel is not None:
            panel = 1.5 * panel - 0.5 * moved
        return split(current), current, panel

    matrix[...] = current
    first_panel = jnp.where(panel_eye, 1.5, 0.0) - 0.5 * matrix[rows_of, :]
    parts, current, _ = advance(split(current), current, None, square)
    parts, current, panel = advance(parts, current, first_panel)
    parts, current, panel = advance(parts, current, panel)
    panel = 1.5 * panel - 0.5 * narrow(split(panel), parts)
    last = narrow(split(panel), parts)
    last = 1.5 * last - 0.5 * narrow(split(last), parts)
    last = 1.5 * last - 0.5 * narrow(split(last), parts)
    panel = 1.5 * panel - 0.5 * last
    factor = (panel * jnp.sqrt(total_rows * scale / frob_norm)).astype(BF16)
    keep = flag_ref[0:1, pl.ds(pl.multiple_of(s * 128, 128), 128)]
    chunk = 512
    for k in range(rows // chunk):
        block = pl.ds(k * chunk, chunk)
        left = jnp.concatenate([all_ref[k4, block] for k4 in range(4)], axis=1)
        value = lax.dot_general(left, factor, (((1,), (1,)), ((), ())), preferred_element_type=F32)
        result[block] = jnp.where(keep == 1.0, value, all_ref[s, block].astype(F32)).astype(BF16)
        pltpu.make_async_copy(result.at[block], out_ref.at[block], out_sem.at[k]).start()
    for k in range(rows // chunk):
        block = pl.ds(k * chunk, chunk)
        pltpu.make_async_copy(result.at[block], out_ref.at[block], out_sem.at[k]).wait()


def finish(total_rows, blocks, parts, squares, scale, late, everything, flag):
    rows, width = everything.shape[1:]
    return pl.pallas_call(
        functools.partial(finish_kernel, total_rows),
        out_shape=jax.ShapeDtypeStruct((rows, width), BF16),
        in_specs=[VMEM] * 7,
        out_specs=ANY,
        scratch_shapes=[
            pltpu.VMEM((512, 512), F32), pltpu.VMEM((rows, width), BF16),
            pltpu.SemaphoreType.DMA((8,)),
        ],
        compiler_params=pltpu.CompilerParams(vmem_limit_bytes=40 * 2**20),
        name="finish",
    )(blocks, parts, squares, scale, late, everything, flag)


def shards(vectors, active):
    total_rows = float(vectors.shape[0] * lax.axis_size("row"))
    return finish(total_rows, *exchange(total_rows, vectors, active))


def solution(mesh):
    in_specs = (P("row", "state"), P())
    out_specs = P("row", "state")
    return jax.shard_map(shards, mesh=mesh, in_specs=in_specs, out_specs=out_specs, check_vma=False)
```

```python
import functools

import jax
import jax.numpy as jnp
from jax import lax
from jax.experimental import pallas as pl
from jax.experimental.pallas import tpu as pltpu
from jax.sharding import PartitionSpec as P

VECS = 64
MESH = pl.DeviceIdType.MESH
F32 = jnp.float32
BF16 = jnp.bfloat16
ANY = pl.BlockSpec(memory_space=pl.ANY)
VMEM = pl.BlockSpec(memory_space=pltpu.VMEM)

HALF, OWN, CORE, PLANE, PBACK, ZDIM, CBACK, LCORE, LOUT, LBACK, LCBACK = 0, 1, 2, 3, 4, 5, 8, 9, 10, 11, 12
LINK, RELAY, QUARTER, SEMS = 13, 29, 45, 61
CHUNKS = 8
FIRST = 8
PLAN = ((0, 1), (2, 3, 4, 5), (6, 7))
OFFSETS = [(a, b, d) for a in range(4) for b in range(4) for d in range(4)]


def hops(offset):
    return sum(min(v, 4 - v) for v in offset)


def gram(left, right):
    return lax.dot_general(left, right, (((0,), (0,)), ((), ())), preferred_element_type=F32)


def split(value):
    high = value.astype(BF16)
    return high, (value - high.astype(F32)).astype(BF16)


def product(left, right):
    (lh, ll), (rh, rl) = left, right
    return jnp.dot(
        jnp.concatenate([ll, lh, lh], axis=1), jnp.concatenate([rh, rl, rh], axis=0), preferred_element_type=F32
    )


def mirrored(left, right, below=None):
    h = left[0].shape[0] // 2
    upper = [v[:h] for v in left]
    if below is not None:
        upper = [jnp.concatenate(pair, axis=0) for pair in zip(upper, below)]
    top = product(upper, right)
    low = product([v[h:] for v in left], [v[:, h:] for v in right])
    top, rest = top[:h], top[h:]
    return jnp.concatenate([top, jnp.concatenate([top[:, h:].T, low], axis=1)], axis=0), rest


def exchange_kernel(
    total_rows, vec_ref, active_hbm, blocks_ref, parts_ref, squares_ref, scale_ref, late_ref, all_ref, flag_ref,
    early_ref, active, quart, early_got, early_z, early_sum, early_own,
    late_part, late_core, late_sum, late_got, mask, local_sem, send_sem, recv_sem, ready,
):
    s, r = lax.axis_index("state"), lax.axis_index("row")
    zh, c = s // 2, s % 2
    zl, x, y = r // 16, (r // 4) % 4, r % 4
    z = zh * 2 + zl
    other_r = r + 16 * (1 - 2 * zl)
    near = s + 1 - 2 * c
    partner = (near, r)
    far = 2 - 2 * zh
    rows = vec_ref.shape[0]
    quart_rows = rows // 4

    xs = [lax.rem(x + a, 4) * 4 for a in range(4)]
    ys = [lax.rem(y + b, 4) for b in range(4)]
    zs = [lax.rem(z + d, 4) for d in range(4)]
    states = [lax.div(to, 2) * 2 + c for to in zs]
    lows = [lax.rem(to, 2) * 16 for to in zs]
    spots = [[to_x + to_y for to_y in ys] for to_x in xs]

    def device(offset):
        a, b, d = offset
        return (states[d], lows[d] + spots[a][b])

    def x_peer(d):
        return device((d, 0, 0))

    def y_peer(d):
        return device((0, d, 0))

    def z_peer(d):
        return device((0, 0, d))

    def send(src, dst, sem, to, recv=None):
        return pltpu.make_async_remote_copy(
            src_ref=src, dst_ref=dst, send_sem=send_sem.at[sem],
            recv_sem=recv_sem.at[sem if recv is None else recv],
            device_id=to, device_id_type=MESH,
        )

    started = []

    def start(copies, wait=True):
        for copy in copies:
            copy.start()
        if wait:
            started.extend(copies)
        return copies

    def arrive(copies):
        for copy in copies:
            copy.wait_recv()

    flag_copy = pltpu.make_async_copy(active_hbm, active, local_sem.at[1])
    flag_copy.start()
    own = pltpu.make_async_copy(vec_ref, all_ref.at[s], local_sem.at[2])
    own.start()

    barrier = pltpu.get_barrier_semaphore()
    peers = [partner] + [(t, other_r) for t in range(4)] + [z_peer(2)]
    peers += [x_peer(d) for d in (1, 2, 3)] + [y_peer(d) for d in (1, 2, 3)]
    for peer in peers:
        pl.semaphore_signal(barrier, inc=1, device_id=peer, device_id_type=MESH)
    pl.semaphore_wait(barrier, len(peers))

    start([send(vec_ref, all_ref.at[s], OWN, partner)])
    edges = [0, FIRST * quart_rows // 16, quart_rows]
    pieces = [pl.ds(edges[k], edges[k + 1] - edges[k]) for k in (0, 1)]

    def quarter(piece, t, frm):
        return send(
            vec_ref.at[pl.ds(t * quart_rows + edges[piece], edges[piece + 1] - edges[piece])],
            quart.at[frm, pieces[piece]], QUARTER + piece * 4 + t, (t, other_r), recv=QUARTER + piece * 4 + frm,
        )

    for piece in (0, 1):
        start([quarter(piece, t, s) for t in range(4)])
    for d in (1, 2, 3):
        pl.semaphore_signal(ready, inc=1, device_id=x_peer(d), device_id_type=MESH)

    flag_copy.wait()

    def flags(shape, axis, first):
        state = lax.broadcasted_iota(jnp.int32, shape, axis) // VECS + first
        flag = jnp.zeros(shape, F32)
        for k in range(8):
            flag = jnp.where(state == k, active[k].astype(F32), flag)
        return flag

    flag_ref[...] = flags(flag_ref.shape, 1, 0)
    block = (256, 256)
    mask[...] = flags(block, 0, 0) * flags(block, 1, 4)
    early_mask = flags((128, 256), 0, s * 2) * flags((128, 256), 1, zh * 4)

    own.wait()
    send(vec_ref, all_ref.at[near], OWN, partner).wait_recv()
    both = jnp.concatenate([all_ref[s - c], all_ref[s - c + 1]], axis=1)
    total = jnp.where(early_mask == 1.0, gram(all_ref[s], both), 0.0)
    early_sum[...] = total.reshape(16, 8, 256)
    pl.semaphore_wait(ready, 3)
    spot = x * 4 + y
    plane = sorted([(a, b, 0) for a in range(4) for b in range(4) if a or b], key=hops, reverse=True)
    start([
        send(early_sum.at[((x + a) % 4) * 4 + (y + b) % 4], early_got.at[spot], PLANE, device((a, b, 0)))
        for a, b, _ in plane
    ], False)
    early_got[spot] = early_sum[spot]
    fifteen = early_got.at[pl.ds(0, 15)]
    send(fifteen, fifteen, PLANE, partner).wait_recv()
    early_own[...] = jnp.sum(early_got[...], axis=0)
    early_z[z] = early_own[...]
    early_step = start([send(early_own, early_z.at[z], ZDIM + d - 1, z_peer(d)) for d in (1, 2, 3)])

    chunk_rows = 2 * quart_rows // CHUNKS

    def chunk_at(chunk, core, frm):
        part, piece = chunk // (CHUNKS // 2), chunk % (CHUNKS // 2)
        return all_ref.at[far + part, pl.ds((frm * 2 + core) * quart_rows + piece * chunk_rows, chunk_rows)]

    def link(chunk):
        part, piece = chunk // (CHUNKS // 2), chunk % (CHUNKS // 2)
        return [
            send(
                quart.at[2 - 2 * to + part, pl.ds(piece * chunk_rows, chunk_rows)],
                all_ref.at[2 - 2 * to + part, pl.ds(s * quart_rows + piece * chunk_rows, chunk_rows)],
                LINK + chunk * 2 + to, (to * 2 + c, other_r), recv=LINK + chunk * 2 + zh,
            )
            for to in (0, 1)
        ]

    def relay_copies(chunk, core):
        blocks = [chunk_at(chunk, core, frm) for frm in (0, 1)]
        return [send(block, block, RELAY + chunk * 2 + frm, partner) for frm, block in enumerate(blocks)]

    def relay(chunk):
        for frm in (0, 1):
            block = chunk_at(chunk, c, frm)
            send(block, block, LINK + chunk * 2 + frm, partner).wait_recv()
        start(relay_copies(chunk, c))

    for piece in (0, 1):
        arrive([quarter(piece, 0, t) for t in range(4)])
    for chunk in PLAN[0]:
        start(link(chunk))
    left = jnp.concatenate([quart[0], quart[1]], axis=1)
    right = jnp.concatenate([quart[2], quart[3]], axis=1)
    late_part[...] = jnp.where(mask[...] == 1.0, gram(left, right), 0.0)
    step = start([send(late_part.at[pl.ds((1 - c) * 128, 128)], late_core, LCORE, partner)])
    arrive(step)
    total = late_part[pl.ds(pl.multiple_of(c * 128, 128), 128), :] + late_core[...]
    for k in (0, 1):
        late_sum[:, k] = total[:, k * 128:(k + 1) * 128].reshape(16, 8, 128)
    odd = (x + y + z + c) % 2
    place = x * 16 + y * 4 + z
    outward = sorted([(a, b, d) for a in range(4) for b in range(4) for d in (0, 2)], key=hops, reverse=True)

    owner_z = [[lax.rem(z + d + even, 4) for even in (odd, 1 - odd)] for d in (0, 2)]
    owner_state = [[lax.div(to, 2) * 2 + c for to in pair] for pair in owner_z]
    owner_low = [[lax.rem(to, 2) * 16 for to in pair] for pair in owner_z]
    owner_half = [[lax.div(to, 2) for to in pair] for pair in owner_z]

    def scatter(offset):
        a, b, d = offset
        k, even, spot_to = d // 2, (a + b) % 2, spots[a][b]
        send(
            late_sum.at[spot_to, owner_half[k][even]], late_got.at[place], LOUT,
            (owner_state[k][even], owner_low[k][even] + spot_to),
        ).start()

    for offset in outward:
        if offset == (0, 0, 0):
            pl.when(odd == 1)(functools.partial(scatter, offset))
        else:
            scatter(offset)
    for chunk in PLAN[1]:
        start(link(chunk))
    arrive(early_step)
    early_ref[c, spot, 0] = early_z[0] + early_z[1]
    early_ref[c, spot, 1] = early_z[2] + early_z[3]
    start([send(early_ref.at[c, spot], early_ref.at[c, spot], PBACK, device(offset)) for offset in plane], False)
    for chunk in PLAN[0]:
        relay(chunk)

    here = (c, x * 4 + y, z // 2)

    @pl.when(odd == 0)
    def _():
        late_got[place] = late_sum[x * 4 + y, z // 2]
        whole = late_got.at[pl.ds(0, 63)]
        send(whole, whole, LOUT, partner).wait_recv()
        late_ref[here] = jnp.sum(late_got[...], axis=0)
        for offset in sorted(OFFSETS[1:], key=hops, reverse=True):
            send(late_ref.at[here], late_ref.at[here], LBACK, device(offset)).start()

    for chunk in PLAN[2]:
        start(link(chunk))
    for chunk in PLAN[1]:
        relay(chunk)
    fifteen = early_ref.at[c, pl.ds(0, 15)]
    send(fifteen, fifteen, PBACK, partner).wait_recv()
    early_step = start([send(early_ref.at[c], early_ref.at[c], CBACK, partner)])

    arrive(early_step)
    diagonal = lax.broadcasted_iota(jnp.int32, (256, 256), 0) == lax.broadcasted_iota(jnp.int32, (256, 256), 1)
    values = []
    for k in (0, 1):
        idle = diagonal & (flag_ref[0:1, k * 256:k * 256 + 256] == 0.0)
        values.append(early_ref[:, :, k].reshape(256, 256) + jnp.where(idle, total_rows, 0.0))
    largest = jnp.maximum(*[jnp.max(value, keepdims=True) for value in values])
    scale_ref[...] = jnp.broadcast_to(1.0 / largest, scale_ref.shape)
    for k in (0, 1):
        value = values[k] * scale_ref[0:1, 0:1]
        high, low = split(value)
        blocks_ref[k] = value
        parts_ref[0, k] = high
        parts_ref[1, k] = low
        squares_ref[k] = product((high, low), (high, low))

    @pl.when(odd == 0)
    def _():
        gathered = late_got.at[pl.ds(0, 31)]
        send(gathered, gathered, LBACK, partner).wait_recv()

    @pl.when(odd == 1)
    def _():
        gathered = late_got.at[pl.ds(0, 32)]
        send(gathered, gathered, LBACK, partner).wait_recv()

    step = start([send(late_ref.at[c], late_ref.at[c], LCBACK, partner)])
    for chunk in PLAN[2]:
        relay(chunk)
    arrive(step)
    for chunk in range(CHUNKS):
        arrive(relay_copies(chunk, 1 - c))

    @pl.when(odd == 0)
    def _():
        out, back = late_got.at[pl.ds(0, 31)], late_got.at[pl.ds(0, 63)]
        send(out, out, LOUT, partner).wait_send()
        send(back, back, LBACK, partner).wait_send()

    @pl.when(odd == 1)
    def _():
        out = late_got.at[pl.ds(0, 32)]
        send(out, out, LOUT, partner).wait_send()

    send(fifteen, fifteen, PBACK, partner).wait_send()
    fifteen = early_got.at[pl.ds(0, 15)]
    send(fifteen, fifteen, PLANE, partner).wait_send()
    for copy in started:
        copy.wait_send()


def exchange(total_rows, vectors, active):
    rows, width = vectors.shape
    hbm = pl.BlockSpec(memory_space=pltpu.HBM)
    return pl.pallas_call(
        functools.partial(exchange_kernel, total_rows),
        out_shape=(
            jax.ShapeDtypeStruct((2, 256, 256), F32),
            jax.ShapeDtypeStruct((2, 2, 256, 256), BF16),
            jax.ShapeDtypeStruct((2, 256, 256), F32),
            jax.ShapeDtypeStruct((8, 128), F32),
            jax.ShapeDtypeStruct((2, 16, 2, 8, 128), F32),
            jax.ShapeDtypeStruct((4, rows, width), BF16),
            jax.ShapeDtypeStruct((8, 512), F32),
        ),
        in_specs=[hbm, hbm],
        out_specs=(VMEM,) * 7,
        scratch_shapes=[
            pltpu.VMEM((2, 16, 2, 8, 256), F32),
            pltpu.SMEM((8,), jnp.int32),
            pltpu.VMEM((4, rows // 4, width), BF16), pltpu.VMEM((16, 8, 256), F32),
            pltpu.VMEM((4, 8, 256), F32), pltpu.VMEM((16, 8, 256), F32), pltpu.VMEM((8, 256), F32),
            pltpu.VMEM((256, 256), F32), pltpu.VMEM((128, 256), F32), pltpu.VMEM((16, 2, 8, 128), F32),
            pltpu.VMEM((64, 8, 128), F32), pltpu.VMEM((256, 256), F32),
            pltpu.SemaphoreType.DMA((3,)), pltpu.SemaphoreType.DMA((SEMS,)), pltpu.SemaphoreType.DMA((SEMS,)),
            pltpu.SemaphoreType.REGULAR,
        ],
        compiler_params=pltpu.CompilerParams(
            collective_id=0, has_side_effects=True, vmem_limit_bytes=24 * 2**20
        ),
        name="exchange",
    )(*[pltpu.with_memory_space_constraint(v, pltpu.HBM) for v in (vectors, active)])


def narrow(left, right):
    (lh, ll), (rh, rl) = left, right
    rows = lh.shape[0]
    both = jnp.dot(jnp.concatenate([lh, ll], axis=0), rh, preferred_element_type=F32)
    return both[:rows] + (both[rows:] + jnp.dot(lh, rl, preferred_element_type=F32))


def finish_kernel(
    total_rows, blocks_ref, parts_ref, squares_ref, scale_ref, late_ref, all_ref, flag_ref, out_ref, matrix, result, out_sem,
):
    s = lax.axis_index("state")
    rows = all_ref.shape[1]
    cols = matrix.shape[0]
    scale = scale_ref[0:1, 0:1]
    cross = jnp.concatenate([late_ref[:, :, k].reshape(256, 128) for k in (0, 1)], axis=1) * scale
    turned = cross.T
    one, two = blocks_ref[0], blocks_ref[1]
    frob_norm = jnp.sqrt(
        jnp.sum(one * one, keepdims=True) + jnp.sum(two * two, keepdims=True) + 2.0 * jnp.sum(cross * cross, keepdims=True)
    )
    inverse_norm = 1.0 / frob_norm
    cross_parts, turned_parts = split(cross), split(turned)
    corner = product(
        [jnp.concatenate([parts_ref[k, 0], cross_parts[k]], axis=1) for k in (0, 1)],
        [jnp.concatenate([cross_parts[k], parts_ref[k, 1]], axis=0) for k in (0, 1)],
    )
    upper = squares_ref[0] + product(cross_parts, turned_parts)
    lower = squares_ref[1] + product(turned_parts, cross_parts)

    def whole(first, second, third, fourth):
        return jnp.concatenate(
            [jnp.concatenate([first, second], axis=1), jnp.concatenate([third, fourth], axis=1)], axis=0
        )

    current = whole(one, cross, turned, two) * inverse_norm
    square = whole(upper, corner, corner.T, lower) * inverse_norm * inverse_norm
    rows_of = pl.ds(pl.multiple_of(s * 128, 128), 128)
    panel_eye = lax.broadcasted_iota(jnp.int32, (128, cols), 0) + s * 128 == lax.broadcasted_iota(jnp.int32, (128, cols), 1)

    def advance(parts, current, panel, square=None):
        if square is None:
            square, moved = mirrored(parts, parts, split(panel))
        first = 1.5 * current - 0.5 * square
        current = 1.5 * first - 0.5 * mirrored(split(first), parts)[0]
        if panel is not None:
            panel = 1.5 * panel - 0.5 * moved
        return split(current), current, panel

    matrix[...] = current
    first_panel = jnp.where(panel_eye, 1.5, 0.0) - 0.5 * matrix[rows_of, :]
    parts, current, _ = advance(split(current), current, None, square)
    parts, current, panel = advance(parts, current, first_panel)
    parts, current, panel = advance(parts, current, panel)
    panel = 1.5 * panel - 0.5 * narrow(split(panel), parts)
    last = narrow(split(panel), parts)
    last = 1.5 * last - 0.5 * narrow(split(last), parts)
    last = 1.5 * last - 0.5 * narrow(split(last), parts)
    panel = 1.5 * panel - 0.5 * last
    factor = (panel * jnp.sqrt(total_rows * scale / frob_norm)).astype(BF16)
    keep = flag_ref[0:1, pl.ds(pl.multiple_of(s * 128, 128), 128)]
    chunk = 512
    for k in range(rows // chunk):
        block = pl.ds(k * chunk, chunk)
        left = jnp.concatenate([all_ref[k4, block] for k4 in range(4)], axis=1)
        value = lax.dot_general(left, factor, (((1,), (1,)), ((), ())), preferred_element_type=F32)
        result[block] = jnp.where(keep == 1.0, value, all_ref[s, block].astype(F32)).astype(BF16)
        pltpu.make_async_copy(result.at[block], out_ref.at[block], out_sem.at[k]).start()
    for k in range(rows // chunk):
        block = pl.ds(k * chunk, chunk)
        pltpu.make_async_copy(result.at[block], out_ref.at[block], out_sem.at[k]).wait()


def finish(total_rows, blocks, parts, squares, scale, late, everything, flag):
    rows, width = everything.shape[1:]
    return pl.pallas_call(
        functools.partial(finish_kernel, total_rows),
        out_shape=jax.ShapeDtypeStruct((rows, width), BF16),
        in_specs=[VMEM] * 7,
        out_specs=ANY,
        scratch_shapes=[
            pltpu.VMEM((512, 512), F32), pltpu.VMEM((rows, width), BF16),
            pltpu.SemaphoreType.DMA((8,)),
        ],
        compiler_params=pltpu.CompilerParams(
            vmem_limit_bytes=40 * 2**20
        ),
        name="finish",
    )(blocks, parts, squares, scale, late, everything, flag)


def shards(vectors, active):
    total_rows = float(vectors.shape[0] * lax.axis_size("row"))
    return finish(total_rows, *exchange(total_rows, vectors, active))


def solution(mesh):
    in_specs = (P("row", "state"), P())
    out_specs = P("row", "state")
    return jax.shard_map(shards, mesh=mesh, in_specs=in_specs, out_specs=out_specs, check_vma=False)
```
